32 devices in a mesh: chan: 8 (over y, x, core), tm: 4 (over z).
Axes of the slice: x: 2, y: 2, z: 4, core: 2. Of those that a mesh axis runs over, the one named last changes fastest.
Arguments:
- traces: bfloat16 [1024, 8, 4096], P('chan', 'tm'), may hold values from -6 to 6
- pair_blocks: int32 [32, 2], P('chan'), may hold values from 0 to 7, as said below
- pair_count: int32 [8], P('chan'), may hold values from 1 to 4, as said below
Outputs:
- stacks: float32 [4096, 2048], P(('chan', 'tm'))
The draws below stay inside these ranges and needn't reach their ends.
Inputs may be any that keep to these rules, and one draw needn't show every extreme that they name: `pair_blocks`: each owner's pairs use blocks at most 2 blocks away from the owner's own block index; the second block lies 1 to 4 blocks after the first; every owner's first slot pairs its lowest with its highest reachable block. `pair_count`: some owner has all slots live.
All inputs are finite; a program needn't handle non-finite values.
Results may differ from the reference program's by a relative error of at most 0.0052.
Values may be sent and summed in bfloat16 or wider, within the bound.
No kernel may reach another device: no remote copies, remote signals or barrier semaphores. Data moves between devices by JAX's collectives and lax.ppermute only.
A program may use at most 192 MiB of HBM per device.

```python
import math
import jax
import jax.numpy as jnp
from jax import lax

NS = 4096
FB = 1024
F_LO = 64
LAGS = 2048
CHAN_BLK = 128
REACH = 2
PB_DEV = 4
BLOCKS = 8
CHANNELS = 1024
SPANS = 8
PAIR_ROWS = 4096


def draw_pair_blocks(key, part):
    slot_rows = lax.iota(jnp.int32, BLOCKS * PB_DEV)
    owners = slot_rows // PB_DEV
    slots = slot_rows % PB_DEV
    lowest = jnp.maximum(owners - REACH, 0)
    highest = jnp.minimum(owners + REACH, BLOCKS - 1)
    key_first, key_second = jax.random.split(jax.random.fold_in(key, 11))
    first_pick = lowest + jax.random.randint(key_first, slot_rows.shape, 0, 4 * REACH + 1) % (highest - lowest)
    second_pick = jnp.minimum(first_pick + jax.random.randint(key_second, slot_rows.shape, 1, 2 * REACH + 1), highest)
    first_pick = jnp.where(slots == 0, lowest, first_pick)
    second_pick = jnp.where(slots == 0, highest, second_pick)
    return jnp.stack([first_pick, second_pick], axis=1).astype(jnp.int32)


def draw_pair_count(key, part):
    key_counts, key_full = jax.random.split(jax.random.fold_in(key, 23))
    counts = jax.random.randint(key_counts, (BLOCKS,), 1, PB_DEV + 1)
    full_owner = jax.random.randint(key_full, (), 0, BLOCKS)
    return jnp.where(lax.iota(jnp.int32, BLOCKS) == full_owner, PB_DEV, counts).astype(jnp.int32)


def block_scale(key, extent, cuts, smallest, largest):
    def one(dim, blocks):
        draws = jax.random.uniform(jax.random.fold_in(jax.random.fold_in(key, 6), dim), (blocks,), jnp.float32, smallest / len(cuts), largest / len(cuts))
        return jnp.repeat(jnp.exp(draws), extent[dim] // blocks).reshape((-1,) + (1,) * (len(extent) - dim - 1))

    loudness = one(*cuts[0])
    for cut in cuts[1:]:
        loudness = loudness * one(*cut)
    return loudness


def gaussian(key, shape, spread, most, shards=(), held_as=jnp.bfloat16):
    result = spread * jax.random.normal(key, shape, jnp.float32)
    if shards:
        result = result * block_scale(key, shape, shards, -0.22, 0.18)
    return jnp.clip(result, -most, most).astype(held_as)


def setup_inputs(seed: int = 0) -> dict:
    splits = jax.random.split(jax.random.key(seed), 4)
    return {
        "traces": gaussian(splits[0], (CHANNELS, SPANS, NS), 1.0, 6.0, ((0, 8), (1, 4))),
        "pair_blocks": draw_pair_blocks(jax.random.fold_in(splits[3], 71), 0),
        "pair_count": draw_pair_count(jax.random.fold_in(splits[3], 71), 0),
    }


def forward_table(first_bin, bin_count, length):
    frequency = first_bin + lax.iota(jnp.int32, bin_count)
    samples = lax.iota(jnp.int32, length)
    phase_angle = (samples[:, None] * frequency[None, :] % length).astype(jnp.float32) * (2.0 * math.pi / length)
    return jnp.concatenate([jnp.cos(phase_angle), -jnp.sin(phase_angle)], axis=1).astype(jnp.bfloat16)

def inverse_table(first_bin, bin_count, length, lag_first, lag_count):
    frequency = first_bin + lax.iota(jnp.int32, bin_count)
    lag_values = lag_first + lax.iota(jnp.int32, lag_count)
    phase_angle = (frequency[:, None] * lag_values[None, :] % length).astype(jnp.float32) * (2.0 * math.pi / length)
    return jnp.concatenate([jnp.cos(phase_angle), -jnp.sin(phase_angle)], axis=0)

def whiten(spectrum, bin_count):
    mean_power = lax.optimization_barrier(jnp.sum(spectrum * spectrum, axis=1, keepdims=True)) / bin_count
    return (spectrum * lax.rsqrt(mean_power + 1e-06)).astype(jnp.bfloat16)

def cross_pair(first_block, second_block, bin_count):
    real_a = first_block[..., :bin_count]
    imag_a = first_block[..., bin_count:]
    real_b = second_block[..., :bin_count]
    imag_b = second_block[..., bin_count:]
    cross_real = lax.optimization_barrier(jnp.sum(real_a * real_b + imag_a * imag_b, axis=1))
    cross_imag = lax.optimization_barrier(jnp.sum(imag_a * real_b - real_a * imag_b, axis=1))
    return jnp.concatenate([cross_real, cross_imag], axis=1)

def reference(traces, pair_blocks, pair_count):
    basis = forward_table(F_LO, FB, NS)
    grouped = traces.reshape(BLOCKS, CHAN_BLK, SPANS, NS)

    def transform_block(samples):
        spectrum = jnp.dot(samples.reshape(CHAN_BLK * SPANS, NS), basis, preferred_element_type=jnp.float32)
        return whiten(spectrum, FB).reshape(CHAN_BLK, SPANS, 2 * FB)
    white = lax.map(transform_block, grouped)
    slot_rows = lax.iota(jnp.int32, BLOCKS * PB_DEV)
    owners = slot_rows // PB_DEV
    alive = (slot_rows % PB_DEV < pair_count[owners]).astype(jnp.float32)

    def cross_slot(inputs):
        pair_row, alive_value = inputs
        first_block = white[pair_row[0]].astype(jnp.float32)
        second_block = white[pair_row[1]].astype(jnp.float32)
        return cross_pair(first_block, second_block, FB) * alive_value
    cross = lax.map(cross_slot, (pair_blocks, alive)).reshape(PAIR_ROWS, 2 * FB)
    inverse = inverse_table(F_LO, FB, NS, -(LAGS // 2), LAGS)
    lag_scale = 1.0 / math.sqrt(FB * SPANS)
    return jnp.dot(cross, inverse, precision=lax.Precision.HIGHEST, preferred_element_type=jnp.float32) * lag_scale
```

```python
import functools
import math

import jax
import jax.numpy as jnp
import numpy as np
from jax import lax
from jax.experimental import pallas as pl
from jax.experimental.pallas import tpu as pltpu
from jax.sharding import PartitionSpec as P

NS = 4096
FB = 1024
F_LO = 64
LAGS = 2048
AXES = ("chan", "tm")

TURN = 4
QUARTER = NS // TURN
GROUP = FB // TURN
STEP = 32
INFO = 128
VMEM = 56 * 1024 * 1024


def bins():
    return np.concatenate([F_LO + g + TURN * np.arange(GROUP) for g in range(TURN)])


def wave(first, second):
    angle = 2.0 * np.pi * (np.multiply.outer(first, second) % NS) / NS
    return np.cos(angle).astype(np.float32), np.sin(angle).astype(np.float32)


def forward_seeds():
    coarse = wave(STEP * np.arange(QUARTER // STEP), bins())
    fine = wave(np.arange(STEP), bins())
    return coarse + fine


def inverse_seeds():
    lags = np.arange(LAGS // 2) - LAGS // 2
    coarse = wave(bins()[::STEP], lags)
    fine = wave(TURN * np.arange(STEP), lags)
    return coarse + fine


def turned(power, cosine, sine):
    return [
        ((1, cosine), (-1, sine)),
        ((-1, sine), (-1, cosine)),
        ((-1, cosine), (1, sine)),
        ((1, sine), (1, cosine)),
    ][power % 4]


def signed_sum(terms):
    total = None
    for sign, term in terms:
        if total is None:
            total = term if sign > 0 else -term
        else:
            total = total + term if sign > 0 else total - term
    return total


def forward_kernel(pairs, count, x, coarse_c, coarse_s, fine_c, fine_s, out, spec, table):
    rows = spec.shape[0]
    slots = pairs.shape[0]
    for g in range(TURN):
        columns = slice(g * GROUP, (g + 1) * GROUP)

        def fill(i, carry, columns=columns):
            c, s = coarse_c[pl.ds(i, 1), columns], coarse_s[pl.ds(i, 1), columns]
            fc, fs = fine_c[:, columns], fine_s[:, columns]
            at = pl.ds(pl.multiple_of(i * STEP, STEP), STEP)
            table[at, :GROUP] = (c * fc - s * fs).astype(jnp.bfloat16)
            table[at, GROUP:] = (s * fc + c * fs).astype(jnp.bfloat16)
            return carry

        lax.fori_loop(0, QUARTER // STEP, fill, 0, unroll=4)
        product = jnp.dot(x[...], table[...], preferred_element_type=jnp.float32)
        parts = [
            turned((F_LO + g) * m, product[m * rows : (m + 1) * rows, :GROUP], product[m * rows : (m + 1) * rows, GROUP:])
            for m in range(TURN)
        ]
        spec[:, columns] = signed_sum([p[0] for p in parts])
        spec[:, FB + g * GROUP : FB + (g + 1) * GROUP] = signed_sum([p[1] for p in parts])
    spectrum = spec[...]
    mean_power = jnp.sum(spectrum * spectrum, axis=1, keepdims=True) / FB
    out[:, : 2 * FB] = (spectrum * lax.rsqrt(mean_power + 1e-06)).astype(jnp.bfloat16)
    lane = lax.broadcasted_iota(jnp.int32, (rows, INFO), 1)
    info = jnp.where(lane == 2 * slots, count[0], 0)
    for slot in range(slots):
        for side in range(2):
            info = jnp.where(lane == 2 * slot + side, pairs[slot, side], info)
    out[:, 2 * FB :] = info.astype(jnp.float32).astype(jnp.bfloat16)


def forward(traces, pair_blocks, pair_count):
    rows = traces.shape[0] * traces.shape[1]
    samples = traces.reshape(rows, TURN, QUARTER).transpose(1, 0, 2).reshape(TURN * rows, QUARTER)
    smem = pl.BlockSpec(memory_space=pltpu.SMEM)
    vmem = pl.BlockSpec(memory_space=pltpu.VMEM)
    return pl.pallas_call(
        forward_kernel,
        out_shape=jax.ShapeDtypeStruct((rows, 2 * FB + INFO), jnp.bfloat16),
        in_specs=[smem, smem] + [vmem] * 5,
        out_specs=vmem,
        scratch_shapes=[pltpu.VMEM((rows, 2 * FB), jnp.float32), pltpu.VMEM((QUARTER, 2 * GROUP), jnp.bfloat16)],
        compiler_params=pltpu.CompilerParams(vmem_limit_bytes=VMEM),
        cost_estimate=pl.CostEstimate(
            flops=2 * rows * NS * 2 * FB, bytes_accessed=2 * rows * (NS + 2 * FB), transcendentals=0
        ),
        name="forward",
    )(pair_blocks, pair_count, samples, *forward_seeds())


def table_kernel(coarse_c, coarse_s, fine_c, fine_s, table_c, table_s):
    def fill(i, carry):
        c, s = coarse_c[pl.ds(i, 1), :], coarse_s[pl.ds(i, 1), :]
        at = pl.ds(pl.multiple_of(i * STEP, STEP), STEP)
        table_c[at, :] = (c * fine_c[...] - s * fine_s[...]).astype(jnp.bfloat16)
        table_s[at, :] = (s * fine_c[...] + c * fine_s[...]).astype(jnp.bfloat16)
        return carry

    lax.fori_loop(0, FB // STEP, fill, 0)


def inverse_tables():
    half = LAGS // 2
    vmem = pl.BlockSpec(memory_space=pltpu.VMEM)
    return pl.pallas_call(
        table_kernel,
        out_shape=[jax.ShapeDtypeStruct((FB, half), jnp.bfloat16)] * 2,
        in_specs=[vmem] * 4,
        out_specs=[vmem] * 2,
        compiler_params=pltpu.CompilerParams(vmem_limit_bytes=VMEM),
        cost_estimate=pl.CostEstimate(flops=8 * FB * half, bytes_accessed=4 * FB * half, transcendentals=0),
        name="inverse_tables",
    )(*inverse_seeds())


def cross_kernel(slots, groups, w, out, total, info_v, info_s, sem):
    owners = w.shape[0] // groups
    half = out.shape[1]
    for owner in range(owners):
        tail = w[owner * groups, :, 2 * half :].astype(jnp.float32)
        info_v[owner : owner + 1, :] = tail[:1, :].astype(jnp.int32)
    copy = pltpu.make_async_copy(info_v, info_s, sem)
    copy.start()
    copy.wait()
    lanes = 256

    def one(pair, carry):
        owner, slot = pair // slots, pair % slots
        first = pl.ds(info_s[owner, 2 * slot] * groups, groups)
        second = pl.ds(info_s[owner, 2 * slot + 1] * groups, groups)
        alive = slot < info_s[owner, 2 * slots]
        at_re = pl.ds(pl.multiple_of(pair * 16, 16), 8)
        at_im = pl.ds(pl.multiple_of(pair * 16 + 8, 8), 8)

        @pl.when(alive)
        def _():
            for offset in range(0, half, lanes):
                re = slice(offset, offset + lanes)
                im = slice(half + offset, half + offset + lanes)
                re_a, im_a = w[first, :, re].astype(jnp.float32), w[first, :, im].astype(jnp.float32)
                re_b, im_b = w[second, :, re].astype(jnp.float32), w[second, :, im].astype(jnp.float32)
                sum_re = jnp.sum(re_a * re_b + im_a * im_b, axis=0)
                sum_im = jnp.sum(im_a * re_b - re_a * im_b, axis=0)
                for k in range(0, lanes, 128):
                    total[(offset + k) // 128, at_re, :] = sum_re[:, k : k + 128]
                    total[(offset + k) // 128, at_im, :] = sum_im[:, k : k + 128]

        @pl.when(jnp.logical_not(alive))
        def _():
            for k in range(half // 128):
                total[k, at_re, :] = jnp.zeros((8, 128), jnp.float32)
                total[k, at_im, :] = jnp.zeros((8, 128), jnp.float32)

        return carry

    lax.fori_loop(0, owners * slots, one, 0)
    count = out.shape[0]
    for k in range(half // 128):
        even, odd = total[k, pl.ds(0, count, stride=2), :], total[k, pl.ds(1, count, stride=2), :]
        out[:, k * 128 : (k + 1) * 128] = (even + odd).astype(jnp.bfloat16)


def cross_fast(received, slots, groups):
    owners = received.shape[0] // groups
    half = (received.shape[2] - INFO) // 2
    vmem = pl.BlockSpec(memory_space=pltpu.VMEM)
    rows = owners * slots * 8
    return pl.pallas_call(
        functools.partial(cross_kernel, slots, groups),
        out_shape=jax.ShapeDtypeStruct((rows, half), jnp.bfloat16),
        in_specs=[vmem],
        out_specs=vmem,
        scratch_shapes=[
            pltpu.VMEM((half // 128, 2 * rows, 128), jnp.float32),
            pltpu.VMEM((owners, INFO), jnp.int32),
            pltpu.SMEM((owners, INFO), jnp.int32),
            pltpu.SemaphoreType.DMA,
        ],
        compiler_params=pltpu.CompilerParams(vmem_limit_bytes=VMEM),
        cost_estimate=pl.CostEstimate(
            flops=8 * rows * 8 * half, bytes_accessed=2 * received.size + 2 * rows * half, transcendentals=0
        ),
        name="cross",
    )(received)


def cross_plain(received, slots, groups, spans):
    half = (received.shape[2] - INFO) // 2
    owners = received.shape[0] // groups
    channels = received.shape[1] // spans
    info = received.reshape(owners, groups, -1, 2 * half + INFO)[:, 0, 0, 2 * half :].astype(jnp.int32)
    pairs = info[:, : 2 * slots].reshape(owners * slots, 2)
    alive = (lax.iota(jnp.int32, slots)[None, :] < info[:, 2 * slots][:, None]).astype(jnp.float32).reshape(-1)
    blocks = received[:, :, : 2 * half].reshape(owners, groups, channels, spans, 2, half)

    def one(inputs):
        pair, live = inputs
        first, second = blocks[pair[0]].astype(jnp.float32), blocks[pair[1]].astype(jnp.float32)
        re_a, im_a, re_b, im_b = first[..., 0, :], first[..., 1, :], second[..., 0, :], second[..., 1, :]
        cross_re = jnp.sum(re_a * re_b + im_a * im_b, axis=(0, 2))
        cross_im = jnp.sum(im_a * re_b - re_a * im_b, axis=(0, 2))
        return (jnp.stack([cross_re, cross_im]) * live).astype(jnp.bfloat16)

    return lax.map(one, (pairs, alive))


def inverse_kernel(scale, y, table_c, table_s, out):
    rows = y.shape[0]
    half = LAGS // 2
    target = lax.broadcasted_iota(jnp.int32, (rows, rows), 0)
    source = lax.broadcasted_iota(jnp.int32, (rows, rows), 1)
    wanted = source // 8 * 4 + source % 4 + source // 4 % 2 * (rows // 2)
    pick = jnp.where(target == wanted, 1.0, 0.0).astype(jnp.bfloat16)
    ordered = jnp.dot(pick, y[...], preferred_element_type=jnp.float32).astype(jnp.bfloat16)
    near, far = [], []
    for g in range(TURN):
        columns = slice(g * GROUP, (g + 1) * GROUP)
        by_c = jnp.dot(ordered[:, columns], table_c[columns, :], preferred_element_type=jnp.float32)
        by_s = jnp.dot(ordered[:, columns], table_s[columns, :], preferred_element_type=jnp.float32)
        straight = by_c[: rows // 2] - by_s[rows // 2 :]
        crossed = by_s[: rows // 2] + by_c[rows // 2 :]
        near.append((1, straight))
        far.append([(1, straight), (-1, crossed), (-1, straight), (1, crossed)][(F_LO + g) % 4])
    out[:, :half] = signed_sum(near) * scale
    out[:, half:] = signed_sum(far) * scale


def inverse(y, table_c, table_s, scale):
    rows = y.shape[0]
    vmem = pl.BlockSpec(memory_space=pltpu.VMEM)
    return pl.pallas_call(
        functools.partial(inverse_kernel, scale),
        out_shape=jax.ShapeDtypeStruct((rows // 2, LAGS), jnp.float32),
        in_specs=[vmem] * 3,
        out_specs=vmem,
        compiler_params=pltpu.CompilerParams(vmem_limit_bytes=VMEM),
        cost_estimate=pl.CostEstimate(
            flops=2 * rows * FB * LAGS, bytes_accessed=2 * FB * LAGS + 2 * rows * LAGS, transcendentals=0
        ),
        name="inverse",
    )(y, table_c, table_s)


def on_device(traces, pair_blocks, pair_count):
    owners, groups = lax.axis_size("chan"), lax.axis_size("tm")
    devices = owners * groups
    block, spans = traces.shape[0], traces.shape[1]
    slots = pair_blocks.shape[0]
    pieces = groups // slots
    channel_parts = min(devices, block // pieces)
    bin_parts = devices // channel_parts
    channels = block // pieces // channel_parts
    bin_share = FB // bin_parts
    scale = 1.0 / math.sqrt(FB * spans * groups)

    white = forward(traces, pair_blocks, pair_count)
    table_c, table_s = inverse_tables()
    simple = pieces == 1 and bin_parts == 1
    if simple:
        sent = white.reshape(devices, channels * spans, 2 * FB + INFO)
    else:
        body = white[:, : 2 * FB].reshape(pieces, channel_parts, channels, spans, 2, bin_parts, bin_share)
        body = body.transpose(1, 5, 0, 2, 3, 4, 6).reshape(devices, pieces * channels * spans, 2 * bin_share)
        tail = jnp.broadcast_to(white[:1, 2 * FB :], body.shape[:2] + (INFO,))
        sent = jnp.concatenate([body, tail], axis=2)
    received = lax.all_to_all(sent, AXES, split_axis=0, concat_axis=0, tiled=True)
    if simple and channels * spans == 8 and spans == 2:
        cross = cross_fast(received, slots, groups).reshape(devices, 8, FB)
    else:
        cross = cross_plain(received, slots, groups, spans)
        cross = cross.reshape(owners, slots, 2, pieces, channels, bin_share).transpose(0, 1, 3, 2, 4, 5)
        cross = cross.reshape(devices, 2 * channels, bin_share)
    own = lax.all_to_all(cross, AXES, split_axis=0, concat_axis=0, tiled=True)
    rows = block // pieces
    if not (simple and channels == 4):
        own = own.reshape(channel_parts, bin_parts, 2, channels, bin_share).transpose(0, 3, 2, 1, 4)
        own = own.reshape(rows // 4, 4, 2, FB).transpose(0, 2, 1, 3)
    return inverse(own.reshape(2 * rows, FB), table_c, table_s, scale)


def solution(mesh):
    return jax.shard_map(
        on_device,
        mesh=mesh,
        in_specs=(P("chan", "tm", None), P("chan", None), P("chan")),
        out_specs=P(("chan", "tm"), None),
        check_vma=False,
    )
```

```python
import functools
import math

import jax
import jax.numpy as jnp
import numpy as np
from jax import lax
from jax.experimental import pallas as pl
from jax.experimental.pallas import tpu as pltpu
from jax.sharding import PartitionSpec as P

NS = 4096
FB = 1024
F_LO = 64
LAGS = 2048
AXES = ("chan", "tm")

TURN = 4
QUARTER = NS // TURN
GROUP = FB // TURN
STEP = 32
VMEM = 24 * 1024 * 1024


def bins():
    return np.concatenate([F_LO + g + TURN * np.arange(GROUP) for g in range(TURN)])


def wave(first, second):
    angle = 2.0 * np.pi * (np.multiply.outer(first, second) % NS) / NS
    return np.cos(angle).astype(np.float32), np.sin(angle).astype(np.float32)


def forward_seeds():
    coarse = wave(STEP * np.arange(QUARTER // STEP), bins())
    fine = wave(np.arange(STEP), bins())
    return np.concatenate(coarse + fine)


def inverse_seeds():
    lags = np.arange(LAGS // 2) - LAGS // 2
    coarse = wave(bins()[::STEP], lags)
    fine = wave(TURN * np.arange(STEP), lags)
    return np.concatenate(coarse + fine)


def forward_kernel(x_hbm, seeds_hbm, out, x, seeds, spec, table, plus, minus, sems):
    rows = spec.shape[0]
    seed_copy = pltpu.make_async_copy(seeds_hbm, seeds, sems.at[0])
    x_copy = pltpu.make_async_copy(x_hbm, x, sems.at[1])
    seed_copy.start()
    x_copy.start()
    seed_copy.wait()
    coarse = QUARTER // STEP
    for g in range(TURN):
        columns = slice(g * GROUP, (g + 1) * GROUP)
        cosine, sine = table.at[g % 2, :, :GROUP], table.at[g % 2, :, GROUP:]
        for i in range(coarse):
            c, s = seeds[i : i + 1, columns], seeds[coarse + i : coarse + i + 1, columns]
            fc, fs = seeds[2 * coarse : 2 * coarse + STEP, columns], seeds[2 * coarse + STEP :, columns]
            at = slice(i * STEP, (i + 1) * STEP)
            cosine[at, :] = (c * fc - s * fs).astype(jnp.bfloat16)
            sine[at, :] = -(s * fc + c * fs).astype(jnp.bfloat16)
        if g == 0:
            x_copy.wait()
            for m in range(TURN):
                samples = slice(m * QUARTER, (m + 1) * QUARTER)
                quarter = x[:, :, samples].reshape(rows, QUARTER)
                plus[:, samples] = quarter
                minus[:, samples] = -quarter
        phases = [(F_LO + g) * m % 4 for m in range(TURN)]
        real = [[(1, cosine), (1, sine), (-1, cosine), (-1, sine)][p] for p in phases]
        imag = [[(1, sine), (-1, cosine), (-1, sine), (1, cosine)][p] for p in phases]
        for start, terms in ((0, real), (FB, imag)):
            left = [
                (plus if sign > 0 else minus)[:, m * QUARTER : (m + 1) * QUARTER] for m, (sign, _) in enumerate(terms)
            ]
            right = [half[...] for _, half in terms]
            spec[:, start + g * GROUP : start + (g + 1) * GROUP] = jnp.dot(
                jnp.concatenate(left, axis=1), jnp.concatenate(right, axis=0), preferred_element_type=jnp.float32
            )
    spectrum = spec[...]
    mean_power = jnp.sum(spectrum * spectrum, axis=1, keepdims=True) / FB
    out[...] = (spectrum * lax.rsqrt(mean_power + 1e-06)).astype(jnp.bfloat16)


def in_hbm(array):
    return pltpu.with_memory_space_constraint(array, pltpu.HBM)


def forward(traces):
    rows = traces.shape[0] * traces.shape[1]
    seeds = forward_seeds()
    return pl.pallas_call(
        forward_kernel,
        out_shape=jax.ShapeDtypeStruct((rows, 2 * FB), jnp.bfloat16),
        in_specs=[pl.BlockSpec(memory_space=pltpu.HBM)] * 2,
        out_specs=pl.BlockSpec(memory_space=pltpu.VMEM),
        scratch_shapes=[
            pltpu.VMEM(traces.shape, jnp.bfloat16),
            pltpu.VMEM(seeds.shape, jnp.float32),
            pltpu.VMEM((rows, 2 * FB), jnp.float32),
            pltpu.VMEM((2, QUARTER, 2 * GROUP), jnp.bfloat16),
            pltpu.VMEM((rows, NS), jnp.bfloat16),
            pltpu.VMEM((rows, NS), jnp.bfloat16),
            pltpu.SemaphoreType.DMA((2,)),
        ],
        compiler_params=pltpu.CompilerParams(vmem_limit_bytes=VMEM),
        cost_estimate=pl.CostEstimate(
            flops=2 * rows * NS * 2 * FB, bytes_accessed=2 * rows * (NS + 2 * FB), transcendentals=0
        ),
        name="forward",
    )(in_hbm(traces), in_hbm(jnp.asarray(seeds)))


def cross_kernel(slots, groups, info, w, out, total):
    owners = w.shape[0] // groups
    half = out.shape[1]
    lanes = 256

    def one(pair, carry):
        owner, slot = pair // slots, pair % slots
        first = pl.ds(info[owner, 2 * slot] * groups, groups)
        second = pl.ds(info[owner, 2 * slot + 1] * groups, groups)
        alive = slot < info[owner, 2 * slots]
        at_re = pl.ds(pl.multiple_of(pair * 16, 16), 8)
        at_im = pl.ds(pl.multiple_of(pair * 16 + 8, 8), 8)

        @pl.when(alive)
        def _():
            for offset in range(0, half, lanes):
                re = slice(offset, offset + lanes)
                im = slice(half + offset, half + offset + lanes)
                re_a, im_a = w[first, :, re].astype(jnp.float32), w[first, :, im].astype(jnp.float32)
                re_b, im_b = w[second, :, re].astype(jnp.float32), w[second, :, im].astype(jnp.float32)
                sum_re = jnp.sum(re_a * re_b + im_a * im_b, axis=0)
                sum_im = jnp.sum(im_a * re_b - re_a * im_b, axis=0)
                for k in range(0, lanes, 128):
                    total[(offset + k) // 128, at_re, :] = sum_re[:, k : k + 128]
                    total[(offset + k) // 128, at_im, :] = sum_im[:, k : k + 128]

        @pl.when(jnp.logical_not(alive))
        def _():
            for k in range(half // 128):
                total[k, at_re, :] = jnp.zeros((8, 128), jnp.float32)
                total[k, at_im, :] = jnp.zeros((8, 128), jnp.float32)

        return carry

    lax.fori_loop(0, owners * slots, one, 0)
    count = out.shape[0]
    for k in range(half // 128):
        even, odd = total[k, pl.ds(0, count, stride=2), :], total[k, pl.ds(1, count, stride=2), :]
        out[:, k * 128 : (k + 1) * 128] = (even + odd).astype(jnp.bfloat16)


def cross_fast(received, info, slots, groups):
    owners = received.shape[0] // groups
    half = received.shape[2] // 2
    vmem = pl.BlockSpec(memory_space=pltpu.VMEM)
    rows = owners * slots * 8
    return pl.pallas_call(
        functools.partial(cross_kernel, slots, groups),
        out_shape=jax.ShapeDtypeStruct((rows, half), jnp.bfloat16),
        in_specs=[pl.BlockSpec(memory_space=pltpu.SMEM), vmem],
        out_specs=vmem,
        scratch_shapes=[pltpu.VMEM((half // 128, 2 * rows, 128), jnp.float32)],
        compiler_params=pltpu.CompilerParams(vmem_limit_bytes=VMEM),
        cost_estimate=pl.CostEstimate(
            flops=8 * rows * 8 * half, bytes_accessed=2 * received.size + 2 * rows * half, transcendentals=0
        ),
        name="cross",
    )(info, received)


def cross_plain(received, info, slots, groups, spans):
    half = received.shape[2] // 2
    owners = received.shape[0] // groups
    channels = received.shape[1] // spans
    pairs = info[:, : 2 * slots].reshape(owners * slots, 2)
    alive = (lax.iota(jnp.int32, slots)[None, :] < info[:, 2 * slots][:, None]).astype(jnp.float32).reshape(-1)
    blocks = received.reshape(owners, groups, channels, spans, 2, half)

    def one(inputs):
        pair, live = inputs
        first, second = blocks[pair[0]].astype(jnp.float32), blocks[pair[1]].astype(jnp.float32)
        re_a, im_a, re_b, im_b = first[..., 0, :], first[..., 1, :], second[..., 0, :], second[..., 1, :]
        cross_re = jnp.sum(re_a * re_b + im_a * im_b, axis=(0, 2))
        cross_im = jnp.sum(im_a * re_b - re_a * im_b, axis=(0, 2))
        return (jnp.stack([cross_re, cross_im]) * live).astype(jnp.bfloat16)

    return lax.map(one, (pairs, alive))


def every_owner(row):
    owners = lax.axis_size("chan")
    ring = row
    while ring.shape[0] < owners:
        hop = ring.shape[0]
        more = lax.ppermute(ring, "chan", [(source, (source - hop) % owners) for source in range(owners)])
        ring = jnp.concatenate([ring, more])[:owners]
    return jnp.roll(ring, lax.axis_index("chan"), axis=0)


def inverse_kernel(scale, y, seeds, out_hbm, out, ordered, table, sem):
    rows = y.shape[0]
    half = LAGS // 2
    coarse = FB // STEP
    lanes = 256
    target = lax.broadcasted_iota(jnp.int32, (rows, rows), 0)
    source = lax.broadcasted_iota(jnp.int32, (rows, rows), 1)
    channel, part = source // 8 * 4 + source % 4, source // 4 % 2
    first = (target < rows // 2) & (target == channel)
    second = target == channel + rows // 2
    for g in range(TURN):
        columns = slice(g * GROUP, (g + 1) * GROUP)
        sign, swap = [(1, 0), (-1, 1), (-1, 0), (1, 1)][(F_LO + g) % 4]
        for meets in range(2):
            turned = (-sign if swap and meets else sign) * jnp.where(part == (meets ^ swap), 1.0, 0.0)
            pick = jnp.where(first, jnp.where(part == meets, 1.0, 0.0), jnp.where(second, turned, 0.0))
            ordered[:, meets * FB + g * GROUP : meets * FB + (g + 1) * GROUP] = jnp.dot(
                pick.astype(jnp.bfloat16), y[:, columns], preferred_element_type=jnp.float32
            ).astype(jnp.bfloat16)
    copies = []
    for k, offset in enumerate(range(0, half, lanes)):
        columns = slice(offset, offset + lanes)
        fc, fs = seeds[2 * coarse : 2 * coarse + STEP, columns], seeds[2 * coarse + STEP :, columns]
        for i in range(coarse):
            c, s = seeds[i : i + 1, columns], seeds[coarse + i : coarse + i + 1, columns]
            table[k % 2, i * STEP : (i + 1) * STEP, :] = (c * fc - s * fs).astype(jnp.bfloat16)
            table[k % 2, FB + i * STEP : FB + (i + 1) * STEP, :] = -(s * fc + c * fs).astype(jnp.bfloat16)
        product = jnp.dot(ordered[...], table[k % 2], preferred_element_type=jnp.float32) * scale
        for side in range(2):
            at = slice(side * half + offset, side * half + offset + lanes)
            out[:, at] = product[side * rows // 2 : (side + 1) * rows // 2]
            copies.append(pltpu.make_async_copy(out.at[:, at], out_hbm.at[:, at], sem.at[2 * k + side]))
            copies[-1].start()
    for copy in copies:
        copy.wait()


def inverse(y, scale):
    rows = y.shape[0]
    seeds = inverse_seeds()
    vmem = pl.BlockSpec(memory_space=pltpu.VMEM)
    return pl.pallas_call(
        functools.partial(inverse_kernel, scale),
        out_shape=jax.ShapeDtypeStruct((rows // 2, LAGS), jnp.float32),
        in_specs=[vmem] * 2,
        out_specs=pl.BlockSpec(memory_space=pltpu.HBM),
        scratch_shapes=[
            pltpu.VMEM((rows // 2, LAGS), jnp.float32),
            pltpu.VMEM((rows, 2 * FB), jnp.bfloat16),
            pltpu.VMEM((2, 2 * FB, 256), jnp.bfloat16),
            pltpu.SemaphoreType.DMA((LAGS // 256,)),
        ],
        compiler_params=pltpu.CompilerParams(vmem_limit_bytes=VMEM),
        cost_estimate=pl.CostEstimate(
            flops=2 * rows * FB * LAGS, bytes_accessed=2 * rows * FB + 2 * rows * LAGS, transcendentals=0
        ),
        name="inverse",
    )(y, jnp.asarray(seeds))


def on_device(traces, pair_blocks, pair_count):
    owners, groups = lax.axis_size("chan"), lax.axis_size("tm")
    devices = owners * groups
    block, spans = traces.shape[0], traces.shape[1]
    slots = pair_blocks.shape[0]
    pieces = groups // slots
    channel_parts = min(devices, block // pieces)
    bin_parts = devices // channel_parts
    channels = block // pieces // channel_parts
    bin_share = FB // bin_parts
    scale = 1.0 / math.sqrt(FB * spans * groups)

    white = forward(traces)
    simple = pieces == 1 and bin_parts == 1
    if simple:
        sent = white.reshape(devices, channels * spans, 2 * FB)
    else:
        sent = white.reshape(pieces, channel_parts, channels, spans, 2, bin_parts, bin_share)
        sent = sent.transpose(1, 5, 0, 2, 3, 4, 6).reshape(devices, pieces * channels * spans, 2 * bin_share)
    received = lax.all_to_all(sent, AXES, split_axis=0, concat_axis=0, tiled=True)
    row = jnp.concatenate([pair_blocks.reshape(1, 2 * slots), pair_count.reshape(1, 1)], axis=1)
    info = every_owner(lax.optimization_barrier((row, white))[0])
    if simple and channels * spans == 8 and spans == 2:
        cross = cross_fast(received, info, slots, groups).reshape(devices, 8, FB)
    else:
        cross = cross_plain(received, info, slots, groups, spans)
        cross = cross.reshape(owners, slots, 2, pieces, channels, bin_share).transpose(0, 1, 3, 2, 4, 5)
        cross = cross.reshape(devices, 2 * channels, bin_share)
    own = lax.all_to_all(cross, AXES, split_axis=0, concat_axis=0, tiled=True)
    rows = block // pieces
    if not (simple and channels == 4):
        own = own.reshape(channel_parts, bin_parts, 2, channels, bin_share).transpose(0, 3, 2, 1, 4)
        own = own.reshape(rows // 4, 4, 2, FB).transpose(0, 2, 1, 3)
    return inverse(own.reshape(2 * rows, FB), scale)


def solution(mesh):
    return jax.shard_map(
        on_device,
        mesh=mesh,
        in_specs=(P("chan", "tm", None), P("chan", None), P("chan")),
        out_specs=P(("chan", "tm"), None),
        check_vma=False,
    )
```

```python
import functools
import math

import jax
import jax.numpy as jnp
import numpy as np
from jax import lax
from jax.experimental import pallas as pl
from jax.experimental.pallas import tpu as pltpu
from jax.sharding import PartitionSpec as P

NS = 4096
FB = 1024
F_LO = 64
LAGS = 2048
AXES = ("chan", "tm")

TURN = 4
QUARTER = NS // TURN
GROUP = FB // TURN
STEP = 32
VMEM = 28 * 1024 * 1024


def bins():
    return np.concatenate([F_LO + g + TURN * np.arange(GROUP) for g in range(TURN)])


def wave(first, second):
    angle = 2.0 * np.pi * (np.multiply.outer(first, second) % NS) / NS
    return np.cos(angle).astype(np.float32), np.sin(angle).astype(np.float32)


def forward_seeds():
    coarse = wave(STEP * np.arange(QUARTER // STEP), bins())
    fine = wave(np.arange(STEP), bins())
    return np.concatenate(coarse + fine).reshape(-1, TURN, GROUP).swapaxes(0, 1).copy()


def inverse_seeds():
    lags = np.arange(LAGS // 2) - LAGS // 2
    coarse = wave(bins()[::STEP], lags)
    fine = wave(TURN * np.arange(STEP), lags)
    return np.concatenate(coarse + fine)


def forward_kernel(x_hbm, seeds_hbm, out_hbm, x, seeds, table, left, spec, out, seed_sem, x_sem, out_sem):
    rows, parts = spec.shape[0], x_sem.shape[0]
    channels = x.shape[0] // parts
    seed_copies = [pltpu.make_async_copy(seeds_hbm.at[g], seeds.at[g], seed_sem.at[g]) for g in range(TURN)]
    x_copies = []
    for k in range(parts):
        at = pl.ds(k * channels, channels)
        x_copies.append(pltpu.make_async_copy(x_hbm.at[at], x.at[at], x_sem.at[k]))
    for copy in seed_copies + x_copies:
        copy.start()
    coarse = QUARTER // STEP

    def fill(g):
        seed_copies[g].wait()
        fc, fs = seeds[g, 2 * coarse : 2 * coarse + STEP, :], seeds[g, 2 * coarse + STEP :, :]
        for i in range(coarse):
            c, s = seeds[g, i : i + 1, :], seeds[g, coarse + i : coarse + i + 1, :]
            at = slice(i * STEP, (i + 1) * STEP)
            table[g, at, :GROUP] = (c * fc - s * fs).astype(jnp.bfloat16)
            table[g, at, GROUP:] = -(s * fc + c * fs).astype(jnp.bfloat16)

    early = 4
    for g in range(early):
        fill(g)
    for copy in x_copies:
        copy.wait()
    lanes = 256
    for offset in range(0, QUARTER, lanes):
        into = slice(offset, offset + lanes)
        quarters = []
        for m in range(TURN):
            quarter = x[:, :, m * QUARTER + offset : m * QUARTER + offset + lanes].reshape(rows, lanes)
            left[m, :, into] = quarter
            left[TURN + m, :, into] = -quarter
            quarters.append(quarter.astype(jnp.float32))
        even, odd = quarters[0] + quarters[2], quarters[1] + quarters[3]
        for k, value in enumerate((even + odd, even - odd)):
            high = value.astype(jnp.bfloat16)
            left[2 * TURN + 2 * k, :, into] = high
            left[2 * TURN + 2 * k + 1, :, into] = (value - high.astype(jnp.float32)).astype(jnp.bfloat16)
    power = jnp.zeros((rows, GROUP), jnp.float32)
    for g in range(TURN):
        if g >= early:
            fill(g)
        cosine, sine = table[g, :, :GROUP], table[g, :, GROUP:]
        turn = (F_LO + g) % TURN
        if turn % 2 == 0:
            pair = jnp.concatenate([left[2 * TURN + turn], left[2 * TURN + turn + 1]], axis=1)
            real = jnp.dot(pair, jnp.concatenate([cosine] * 2, axis=0), preferred_element_type=jnp.float32)
            imag = jnp.dot(pair, jnp.concatenate([sine] * 2, axis=0), preferred_element_type=jnp.float32)
        else:
            ahead = (0, 1, TURN + 2, TURN + 3) if turn == 1 else (0, TURN + 1, TURN + 2, 3)
            behind = (0, TURN + 1, TURN + 2, 3) if turn == 1 else (0, 1, TURN + 2, TURN + 3)
            real = jnp.dot(
                jnp.concatenate([left[k] for k in ahead], axis=1),
                jnp.concatenate([cosine, sine] * 2, axis=0),
                preferred_element_type=jnp.float32,
            )
            imag = jnp.dot(
                jnp.concatenate([left[k] for k in behind], axis=1),
                jnp.concatenate([sine, cosine] * 2, axis=0),
                preferred_element_type=jnp.float32,
            )
        spec[:, g * GROUP : (g + 1) * GROUP] = real
        spec[:, FB + g * GROUP : FB + (g + 1) * GROUP] = imag
        power = power + real * real + imag * imag
    scale = lax.rsqrt(jnp.sum(power, axis=1, keepdims=True) / FB + 1e-06)
    out_copies = []
    pieces = out_sem.shape[0]
    for k in range(pieces):
        at = slice(k * rows // pieces, (k + 1) * rows // pieces)
        out[at, :] = (spec[at, :] * scale[at, :]).astype(jnp.bfloat16)
        out_copies.append(pltpu.make_async_copy(out.at[at], out_hbm.at[at], out_sem.at[k]))
        out_copies[-1].start()
    for copy in out_copies:
        copy.wait()


def in_hbm(array):
    return pltpu.with_memory_space_constraint(array, pltpu.HBM)


def forward(traces):
    rows = traces.shape[0] * traces.shape[1]
    seeds = forward_seeds()
    return pl.pallas_call(
        forward_kernel,
        out_shape=jax.ShapeDtypeStruct((rows, 2 * FB), jnp.bfloat16),
        in_specs=[pl.BlockSpec(memory_space=pltpu.HBM)] * 2,
        out_specs=pl.BlockSpec(memory_space=pltpu.HBM),
        scratch_shapes=[
            pltpu.VMEM(traces.shape, jnp.bfloat16),
            pltpu.VMEM(seeds.shape, jnp.float32),
            pltpu.VMEM((TURN, QUARTER, 2 * GROUP), jnp.bfloat16),
            pltpu.VMEM((3 * TURN, rows, QUARTER), jnp.bfloat16),
            pltpu.VMEM((rows, 2 * FB), jnp.float32),
            pltpu.VMEM((rows, 2 * FB), jnp.bfloat16),
            pltpu.SemaphoreType.DMA((TURN,)),
            pltpu.SemaphoreType.DMA((4,)),
            pltpu.SemaphoreType.DMA((4,)),
        ],
        compiler_params=pltpu.CompilerParams(vmem_limit_bytes=VMEM),
        cost_estimate=pl.CostEstimate(
            flops=2 * rows * NS * 2 * FB, bytes_accessed=2 * rows * (NS + 2 * FB), transcendentals=0
        ),
        name="forward",
    )(in_hbm(traces), in_hbm(jnp.asarray(seeds)))


def cross_kernel(slots, groups, info, w, out, total):
    owners = w.shape[0] // groups
    half = out.shape[1]
    lanes = 256

    def one(pair, carry):
        owner, slot = pair // slots, pair % slots
        first = pl.ds(info[owner, 2 * slot] * groups, groups)
        second = pl.ds(info[owner, 2 * slot + 1] * groups, groups)
        alive = slot < info[owner, 2 * slots]
        at_re = pl.ds(pl.multiple_of(pair * 16, 16), 8)
        at_im = pl.ds(pl.multiple_of(pair * 16 + 8, 8), 8)

        @pl.when(alive)
        def _():
            for offset in range(0, half, lanes):
                re = slice(offset, offset + lanes)
                im = slice(half + offset, half + offset + lanes)
                re_a, im_a = w[first, :, re].astype(jnp.float32), w[first, :, im].astype(jnp.float32)
                re_b, im_b = w[second, :, re].astype(jnp.float32), w[second, :, im].astype(jnp.float32)
                sum_re = jnp.sum(re_a * re_b + im_a * im_b, axis=0)
                sum_im = jnp.sum(im_a * re_b - re_a * im_b, axis=0)
                for k in range(0, lanes, 128):
                    total[(offset + k) // 128, at_re, :] = sum_re[:, k : k + 128]
                    total[(offset + k) // 128, at_im, :] = sum_im[:, k : k + 128]

        @pl.when(jnp.logical_not(alive))
        def _():
            for k in range(half // 128):
                total[k, at_re, :] = jnp.zeros((8, 128), jnp.float32)
                total[k, at_im, :] = jnp.zeros((8, 128), jnp.float32)

        return carry

    lax.fori_loop(0, owners * slots, one, 0)
    count = out.shape[0]
    for k in range(half // 128):
        even, odd = total[k, pl.ds(0, count, stride=2), :], total[k, pl.ds(1, count, stride=2), :]
        out[:, k * 128 : (k + 1) * 128] = (even + odd).astype(jnp.bfloat16)


def cross_fast(received, info, slots, groups):
    owners = received.shape[0] // groups
    half = received.shape[2] // 2
    vmem = pl.BlockSpec(memory_space=pltpu.VMEM)
    rows = owners * slots * 8
    return pl.pallas_call(
        functools.partial(cross_kernel, slots, groups),
        out_shape=jax.ShapeDtypeStruct((rows, half), jnp.bfloat16),
        in_specs=[pl.BlockSpec(memory_space=pltpu.SMEM), vmem],
        out_specs=vmem,
        scratch_shapes=[pltpu.VMEM((half // 128, 2 * rows, 128), jnp.float32)],
        compiler_params=pltpu.CompilerParams(vmem_limit_bytes=VMEM),
        cost_estimate=pl.CostEstimate(
            flops=8 * rows * 8 * half, bytes_accessed=2 * received.size + 2 * rows * half, transcendentals=0
        ),
        name="cross",
    )(info, received)


def cross_plain(received, info, slots, groups, spans):
    half = received.shape[2] // 2
    owners = received.shape[0] // groups
    channels = received.shape[1] // spans
    pairs = info[:, : 2 * slots].reshape(owners * slots, 2)
    alive = (lax.iota(jnp.int32, slots)[None, :] < info[:, 2 * slots][:, None]).astype(jnp.float32).reshape(-1)
    blocks = received.reshape(owners, groups, channels, spans, 2, half)

    def one(inputs):
        pair, live = inputs
        first, second = blocks[pair[0]].astype(jnp.float32), blocks[pair[1]].astype(jnp.float32)
        re_a, im_a, re_b, im_b = first[..., 0, :], first[..., 1, :], second[..., 0, :], second[..., 1, :]
        cross_re = jnp.sum(re_a * re_b + im_a * im_b, axis=(0, 2))
        cross_im = jnp.sum(im_a * re_b - re_a * im_b, axis=(0, 2))
        return (jnp.stack([cross_re, cross_im]) * live).astype(jnp.bfloat16)

    return lax.map(one, (pairs, alive))


def every_owner(row):
    owners = lax.axis_size("chan")
    ring = row
    while ring.shape[0] < owners:
        hop = ring.shape[0]
        more = lax.ppermute(ring, "chan", [(source, (source - hop) % owners) for source in range(owners)])
        ring = jnp.concatenate([ring, more])[:owners]
    return jnp.roll(ring, lax.axis_index("chan"), axis=0)


def inverse_kernel(scale, y, seeds, out_hbm, out, ordered, table, sem):
    rows = y.shape[0]
    half = LAGS // 2
    coarse = FB // STEP
    lanes = 256
    target = lax.broadcasted_iota(jnp.int32, (rows, rows), 0)
    source = lax.broadcasted_iota(jnp.int32, (rows, rows), 1)
    wanted = source // 8 * 4 + source % 4 + source // 4 % 2 * (rows // 2)
    pick = jnp.where(target == wanted, 1.0, 0.0).astype(jnp.bfloat16)
    for g in range(TURN):
        columns = slice(g * GROUP, (g + 1) * GROUP)
        moved = jnp.dot(pick, y[:, columns], preferred_element_type=jnp.float32)
        real, imag = moved[: rows // 2], moved[rows // 2 :]
        far = [(real, imag), (-imag, real), (-real, -imag), (imag, -real)][(F_LO + g) % TURN]
        for k, (near_side, far_side) in enumerate(zip((real, imag), far)):
            into = slice(k * FB + g * GROUP, k * FB + (g + 1) * GROUP)
            ordered[: rows // 2, into] = near_side.astype(jnp.bfloat16)
            ordered[rows // 2 :, into] = far_side.astype(jnp.bfloat16)
    copies = []
    for k, offset in enumerate(range(0, half, lanes)):
        columns = slice(offset, offset + lanes)
        fc, fs = seeds[2 * coarse : 2 * coarse + STEP, columns], seeds[2 * coarse + STEP :, columns]
        for i in range(coarse):
            c, s = seeds[i : i + 1, columns], seeds[coarse + i : coarse + i + 1, columns]
            table[k % 2, i * STEP : (i + 1) * STEP, :] = (c * fc - s * fs).astype(jnp.bfloat16)
            table[k % 2, FB + i * STEP : FB + (i + 1) * STEP, :] = -(s * fc + c * fs).astype(jnp.bfloat16)
        product = jnp.dot(ordered[...], table[k % 2], preferred_element_type=jnp.float32) * scale
        for side in range(2):
            at = slice(side * half + offset, side * half + offset + lanes)
            out[:, at] = product[side * rows // 2 : (side + 1) * rows // 2]
            copies.append(pltpu.make_async_copy(out.at[:, at], out_hbm.at[:, at], sem.at[2 * k + side]))
            copies[-1].start()
    for copy in copies:
        copy.wait()


def inverse(y, scale):
    rows = y.shape[0]
    seeds = inverse_seeds()
    vmem = pl.BlockSpec(memory_space=pltpu.VMEM)
    return pl.pallas_call(
        functools.partial(inverse_kernel, scale),
        out_shape=jax.ShapeDtypeStruct((rows // 2, LAGS), jnp.float32),
        in_specs=[vmem] * 2,
        out_specs=pl.BlockSpec(memory_space=pltpu.HBM),
        scratch_shapes=[
            pltpu.VMEM((rows // 2, LAGS), jnp.float32),
            pltpu.VMEM((rows, 2 * FB), jnp.bfloat16),
            pltpu.VMEM((2, 2 * FB, 256), jnp.bfloat16),
            pltpu.SemaphoreType.DMA((LAGS // 256,)),
        ],
        compiler_params=pltpu.CompilerParams(vmem_limit_bytes=VMEM),
        cost_estimate=pl.CostEstimate(
            flops=2 * rows * FB * LAGS, bytes_accessed=2 * rows * FB + 2 * rows * LAGS, transcendentals=0
        ),
        name="inverse",
    )(y, jnp.asarray(seeds))


def on_device(traces, pair_blocks, pair_count):
    owners, groups = lax.axis_size("chan"), lax.axis_size("tm")
    devices = owners * groups
    block, spans = traces.shape[0], traces.shape[1]
    slots = pair_blocks.shape[0]
    pieces = groups // slots
    channel_parts = min(devices, block // pieces)
    bin_parts = devices // channel_parts
    channels = block // pieces // channel_parts
    bin_share = FB // bin_parts
    scale = 1.0 / math.sqrt(FB * spans * groups)

    white = forward(traces)
    simple = pieces == 1 and bin_parts == 1
    if simple:
        sent = white.reshape(devices, channels * spans, 2 * FB)
    else:
        sent = white.reshape(pieces, channel_parts, channels, spans, 2, bin_parts, bin_share)
        sent = sent.transpose(1, 5, 0, 2, 3, 4, 6).reshape(devices, pieces * channels * spans, 2 * bin_share)
    received = lax.all_to_all(sent, AXES, split_axis=0, concat_axis=0, tiled=True)
    row = jnp.concatenate([pair_blocks.reshape(1, 2 * slots), pair_count.reshape(1, 1)], axis=1)
    info = every_owner(lax.optimization_barrier((row, white))[0])
    if simple and channels * spans == 8 and spans == 2:
        cross = cross_fast(received, info, slots, groups).reshape(devices, 8, FB)
    else:
        cross = cross_plain(received, info, slots, groups, spans)
        cross = cross.reshape(owners, slots, 2, pieces, channels, bin_share).transpose(0, 1, 3, 2, 4, 5)
        cross = cross.reshape(devices, 2 * channels, bin_share)
    own = lax.all_to_all(cross, AXES, split_axis=0, concat_axis=0, tiled=True)
    rows = block // pieces
    if not (simple and channels == 4):
        own = own.reshape(channel_parts, bin_parts, 2, channels, bin_share).transpose(0, 3, 2, 1, 4)
        own = own.reshape(rows // 4, 4, 2, FB).transpose(0, 2, 1, 3)
    return inverse(own.reshape(2 * rows, FB), scale)


def solution(mesh):
    return jax.shard_map(
        on_device,
        mesh=mesh,
        in_specs=(P("chan", "tm", None), P("chan", None), P("chan")),
        out_specs=P(("chan", "tm"), None),
        check_vma=False,
    )
```

```python
import functools
import math

import jax
import jax.numpy as jnp
import numpy as np
from jax import lax
from jax.experimental import pallas as pl
from jax.experimental.pallas import tpu as pltpu
from jax.sharding import PartitionSpec as P

NS = 4096
FB = 1024
F_LO = 64
LAGS = 2048
AXES = ("chan", "tm")

TURN = 4
QUARTER = NS // TURN
GROUP = FB // TURN
STEP = 32
VMEM = 28 * 1024 * 1024


def bins():
    return np.concatenate([F_LO + g + TURN * np.arange(GROUP) for g in range(TURN)])


def wave(first, second):
    angle = 2.0 * np.pi * (np.multiply.outer(first, second) % NS) / NS
    return np.cos(angle).astype(np.float32), np.sin(angle).astype(np.float32)


def forward_seeds():
    coarse = wave(STEP * np.arange(QUARTER // STEP), bins())
    fine = wave(np.arange(STEP), bins())
    return np.concatenate(coarse + fine).reshape(-1, TURN, GROUP).swapaxes(0, 1).copy()


def inverse_seeds():
    lags = np.arange(LAGS // 2) - LAGS // 2
    coarse = wave(bins()[::STEP], lags)
    fine = wave(TURN * np.arange(STEP), lags)
    return np.concatenate(coarse + fine)


def forward_kernel(x_hbm, seeds_hbm, out_hbm, x, seeds, table, left, spec, out, seed_sem, x_sem, out_sem):
    rows, parts = spec.shape[0], x_sem.shape[0]
    channels = x.shape[0] // parts
    seed_copies = [pltpu.make_async_copy(seeds_hbm.at[g], seeds.at[g], seed_sem.at[g]) for g in range(TURN)]
    x_copies = []
    for k in range(parts):
        at = pl.ds(k * channels, channels)
        x_copies.append(pltpu.make_async_copy(x_hbm.at[at], x.at[at], x_sem.at[k]))
    for copy in seed_copies[1:2] + x_copies[:1] + seed_copies[3:] + x_copies[1:2] + seed_copies[:1] + x_copies[2:3] + seed_copies[2:3] + x_copies[3:]:
        copy.start()
    coarse = QUARTER // STEP

    def fill(g):
        seed_copies[g].wait()
        fc, fs = seeds[g, 2 * coarse : 2 * coarse + STEP, :], seeds[g, 2 * coarse + STEP :, :]
        for i in range(coarse):
            c, s = seeds[g, i : i + 1, :], seeds[g, coarse + i : coarse + i + 1, :]
            at = slice(i * STEP, (i + 1) * STEP)
            table[g, at, :GROUP] = (c * fc - s * fs).astype(jnp.bfloat16)
            table[g, at, GROUP:] = -(s * fc + c * fs).astype(jnp.bfloat16)

    for g in (1, 3, 0, 2):
        fill(g)
    lanes = QUARTER
    for k, copy in enumerate(x_copies):
        copy.wait()
        here = slice(k * rows // parts, (k + 1) * rows // parts)
        for m in range(TURN):
            quarter = x[k * channels : (k + 1) * channels, :, m * QUARTER : (m + 1) * QUARTER].reshape(rows // parts, QUARTER)
            left[m, here, :] = quarter
            if m:
                left[TURN + m, here, :] = -quarter

    def add_quarters():
        for offset in range(0, QUARTER, lanes):
            into = slice(offset, offset + lanes)
            quarters = [left[m, :, into].astype(jnp.float32) for m in range(TURN)]
            even, odd = quarters[0] + quarters[2], quarters[1] + quarters[3]
            for k, value in enumerate((even + odd, even - odd)):
                high = value.astype(jnp.bfloat16)
                left[2 * TURN + 2 * k, :, into] = high
                left[2 * TURN + 2 * k + 1, :, into] = (value - high.astype(jnp.float32)).astype(jnp.bfloat16)

    power = jnp.zeros((rows, GROUP), jnp.float32)
    for at_g, g in enumerate((1, 3, 0, 2)):
        if g not in (1, 3, 0, 2):
            fill(g)
        if at_g == 2:
            add_quarters()
        cosine, sine = table[g, :, :GROUP], table[g, :, GROUP:]
        turn = (F_LO + g) % TURN
        if turn % 2 == 0:
            pair = jnp.concatenate([left[2 * TURN + turn], left[2 * TURN + turn + 1]], axis=1)
            real = jnp.dot(pair, jnp.concatenate([cosine] * 2, axis=0), preferred_element_type=jnp.float32)
            imag = jnp.dot(pair, jnp.concatenate([sine] * 2, axis=0), preferred_element_type=jnp.float32)
        else:
            ahead = (0, 1, TURN + 2, TURN + 3) if turn == 1 else (0, TURN + 1, TURN + 2, 3)
            behind = (0, TURN + 1, TURN + 2, 3) if turn == 1 else (0, 1, TURN + 2, TURN + 3)
            real = jnp.dot(
                jnp.concatenate([left[k] for k in ahead], axis=1),
                jnp.concatenate([cosine, sine] * 2, axis=0),
                preferred_element_type=jnp.float32,
            )
            imag = jnp.dot(
                jnp.concatenate([left[k] for k in behind], axis=1),
                jnp.concatenate([sine, cosine] * 2, axis=0),
                preferred_element_type=jnp.float32,
            )
        spec[:, g * GROUP : (g + 1) * GROUP] = real
        spec[:, FB + g * GROUP : FB + (g + 1) * GROUP] = imag
        power = power + real * real + imag * imag
    scale = lax.rsqrt(jnp.sum(power, axis=1, keepdims=True) / FB + 1e-06)
    out_copies = []
    pieces = out_sem.shape[0]
    for k in range(pieces):
        at = slice(k * rows // pieces, (k + 1) * rows // pieces)
        out[at, :] = (spec[at, :] * scale[at, :]).astype(jnp.bfloat16)
        out_copies.append(pltpu.make_async_copy(out.at[at], out_hbm.at[at], out_sem.at[k]))
        out_copies[-1].start()
    for copy in out_copies:
        copy.wait()


def in_hbm(array):
    return pltpu.with_memory_space_constraint(array, pltpu.HBM)


def forward(traces):
    rows = traces.shape[0] * traces.shape[1]
    seeds = forward_seeds()
    return pl.pallas_call(
        forward_kernel,
        out_shape=jax.ShapeDtypeStruct((rows, 2 * FB), jnp.bfloat16),
        in_specs=[pl.BlockSpec(memory_space=pltpu.HBM)] * 2,
        out_specs=pl.BlockSpec(memory_space=pltpu.HBM),
        scratch_shapes=[
            pltpu.VMEM(traces.shape, jnp.bfloat16),
            pltpu.VMEM(seeds.shape, jnp.float32),
            pltpu.VMEM((TURN, QUARTER, 2 * GROUP), jnp.bfloat16),
            pltpu.VMEM((3 * TURN, rows, QUARTER), jnp.bfloat16),
            pltpu.VMEM((rows, 2 * FB), jnp.float32),
            pltpu.VMEM((rows, 2 * FB), jnp.bfloat16),
            pltpu.SemaphoreType.DMA((TURN,)),
            pltpu.SemaphoreType.DMA((4,)),
            pltpu.SemaphoreType.DMA((4,)),
        ],
        compiler_params=pltpu.CompilerParams(vmem_limit_bytes=VMEM),
        cost_estimate=pl.CostEstimate(
            flops=2 * rows * NS * 2 * FB, bytes_accessed=2 * rows * (NS + 2 * FB), transcendentals=0
        ),
        name="forward",
    )(in_hbm(traces), in_hbm(jnp.asarray(seeds)))


def cross_kernel(slots, groups, info, w, out, total):
    owners = w.shape[0] // groups
    half = out.shape[1]
    lanes = 256

    def one(pair, carry):
        owner, slot = pair // slots, pair % slots
        first = pl.ds(info[owner, 2 * slot] * groups, groups)
        second = pl.ds(info[owner, 2 * slot + 1] * groups, groups)
        alive = slot < info[owner, 2 * slots]
        at_re = pl.ds(pl.multiple_of(pair * 16, 16), 8)
        at_im = pl.ds(pl.multiple_of(pair * 16 + 8, 8), 8)

        @pl.when(alive)
        def _():
            for offset in range(0, half, lanes):
                re = slice(offset, offset + lanes)
                im = slice(half + offset, half + offset + lanes)
                re_a, im_a = w[first, :, re].astype(jnp.float32), w[first, :, im].astype(jnp.float32)
                re_b, im_b = w[second, :, re].astype(jnp.float32), w[second, :, im].astype(jnp.float32)
                sum_re = jnp.sum(re_a * re_b + im_a * im_b, axis=0)
                sum_im = jnp.sum(im_a * re_b - re_a * im_b, axis=0)
                for k in range(0, lanes, 128):
                    total[(offset + k) // 128, at_re, :] = sum_re[:, k : k + 128]
                    total[(offset + k) // 128, at_im, :] = sum_im[:, k : k + 128]

        @pl.when(jnp.logical_not(alive))
        def _():
            for k in range(half // 128):
                total[k, at_re, :] = jnp.zeros((8, 128), jnp.float32)
                total[k, at_im, :] = jnp.zeros((8, 128), jnp.float32)

        return carry

    lax.fori_loop(0, owners * slots, one, 0)
    count = out.shape[0]
    for k in range(half // 128):
        even, odd = total[k, pl.ds(0, count, stride=2), :], total[k, pl.ds(1, count, stride=2), :]
        out[:, k * 128 : (k + 1) * 128] = (even + odd).astype(jnp.bfloat16)


def cross_fast(received, info, slots, groups):
    owners = received.shape[0] // groups
    half = received.shape[2] // 2
    vmem = pl.BlockSpec(memory_space=pltpu.VMEM)
    rows = owners * slots * 8
    return pl.pallas_call(
        functools.partial(cross_kernel, slots, groups),
        out_shape=jax.ShapeDtypeStruct((rows, half), jnp.bfloat16),
        in_specs=[pl.BlockSpec(memory_space=pltpu.SMEM), vmem],
        out_specs=vmem,
        scratch_shapes=[pltpu.VMEM((half // 128, 2 * rows, 128), jnp.float32)],
        compiler_params=pltpu.CompilerParams(vmem_limit_bytes=VMEM),
        cost_estimate=pl.CostEstimate(
            flops=8 * rows * 8 * half, bytes_accessed=2 * received.size + 2 * rows * half, transcendentals=0
        ),
        name="cross",
    )(info, received)


def cross_plain(received, info, slots, groups, spans):
    half = received.shape[2] // 2
    owners = received.shape[0] // groups
    channels = received.shape[1] // spans
    pairs = info[:, : 2 * slots].reshape(owners * slots, 2)
    alive = (lax.iota(jnp.int32, slots)[None, :] < info[:, 2 * slots][:, None]).astype(jnp.float32).reshape(-1)
    blocks = received.reshape(owners, groups, channels, spans, 2, half)

    def one(inputs):
        pair, live = inputs
        first, second = blocks[pair[0]].astype(jnp.float32), blocks[pair[1]].astype(jnp.float32)
        re_a, im_a, re_b, im_b = first[..., 0, :], first[..., 1, :], second[..., 0, :], second[..., 1, :]
        cross_re = jnp.sum(re_a * re_b + im_a * im_b, axis=(0, 2))
        cross_im = jnp.sum(im_a * re_b - re_a * im_b, axis=(0, 2))
        return (jnp.stack([cross_re, cross_im]) * live).astype(jnp.bfloat16)

    return lax.map(one, (pairs, alive))


def every_owner(row):
    owners = lax.axis_size("chan")
    ring = row
    while ring.shape[0] < owners:
        hop = ring.shape[0]
        more = lax.ppermute(ring, "chan", [(source, (source - hop) % owners) for source in range(owners)])
        ring = jnp.concatenate([ring, more])[:owners]
    return jnp.roll(ring, lax.axis_index("chan"), axis=0)


def inverse_kernel(scale, y, seeds, out_hbm, out, ordered, table, sem):
    rows = y.shape[0]
    half = LAGS // 2
    coarse = FB // STEP
    lanes = 256
    target = lax.broadcasted_iota(jnp.int32, (rows, rows), 0)
    source = lax.broadcasted_iota(jnp.int32, (rows, rows), 1)
    wanted = source // 8 * 4 + source % 4 + source // 4 % 2 * (rows // 2)
    pick = jnp.where(target == wanted, 1.0, 0.0).astype(jnp.bfloat16)
    for g in range(TURN):
        columns = slice(g * GROUP, (g + 1) * GROUP)
        moved = jnp.dot(pick, y[:, columns], preferred_element_type=jnp.float32)
        real, imag = moved[: rows // 2], moved[rows // 2 :]
        far = [(real, imag), (-imag, real), (-real, -imag), (imag, -real)][(F_LO + g) % TURN]
        for k, (near_side, far_side) in enumerate(zip((real, imag), far)):
            into = slice(k * FB + g * GROUP, k * FB + (g + 1) * GROUP)
            ordered[: rows // 2, into] = near_side.astype(jnp.bfloat16)
            ordered[rows // 2 :, into] = far_side.astype(jnp.bfloat16)
    copies = []
    for k, offset in enumerate(range(0, half, lanes)):
        columns = slice(offset, offset + lanes)
        fc, fs = seeds[2 * coarse : 2 * coarse + STEP, columns], seeds[2 * coarse + STEP :, columns]
        for i in range(coarse):
            c, s = seeds[i : i + 1, columns], seeds[coarse + i : coarse + i + 1, columns]
            table[k % 2, i * STEP : (i + 1) * STEP, :] = (c * fc - s * fs).astype(jnp.bfloat16)
            table[k % 2, FB + i * STEP : FB + (i + 1) * STEP, :] = -(s * fc + c * fs).astype(jnp.bfloat16)
        product = jnp.dot(ordered[...], table[k % 2], preferred_element_type=jnp.float32) * scale
        for side in range(2):
            at = slice(side * half + offset, side * half + offset + lanes)
            out[:, at] = product[side * rows // 2 : (side + 1) * rows // 2]
            copies.append(pltpu.make_async_copy(out.at[:, at], out_hbm.at[:, at], sem.at[2 * k + side]))
            copies[-1].start()
    for copy in copies:
        copy.wait()


def inverse(y, scale):
    rows = y.shape[0]
    seeds = inverse_seeds()
    vmem = pl.BlockSpec(memory_space=pltpu.VMEM)
    return pl.pallas_call(
        functools.partial(inverse_kernel, scale),
        out_shape=jax.ShapeDtypeStruct((rows // 2, LAGS), jnp.float32),
        in_specs=[vmem] * 2,
        out_specs=pl.BlockSpec(memory_space=pltpu.HBM),
        scratch_shapes=[
            pltpu.VMEM((rows // 2, LAGS), jnp.float32),
            pltpu.VMEM((rows, 2 * FB), jnp.bfloat16),
            pltpu.VMEM((2, 2 * FB, 256), jnp.bfloat16),
            pltpu.SemaphoreType.DMA((LAGS // 256,)),
        ],
        compiler_params=pltpu.CompilerParams(vmem_limit_bytes=VMEM),
        cost_estimate=pl.CostEstimate(
            flops=2 * rows * FB * LAGS, bytes_accessed=2 * rows * FB + 2 * rows * LAGS, transcendentals=0
        ),
        name="inverse",
    )(y, jnp.asarray(seeds))


def on_device(traces, pair_blocks, pair_count):
    owners, groups = lax.axis_size("chan"), lax.axis_size("tm")
    devices = owners * groups
    block, spans = traces.shape[0], traces.shape[1]
    slots = pair_blocks.shape[0]
    pieces = groups // slots
    channel_parts = min(devices, block // pieces)
    bin_parts = devices // channel_parts
    channels = block // pieces // channel_parts
    bin_share = FB // bin_parts
    scale = 1.0 / math.sqrt(FB * spans * groups)

    white = forward(traces)
    simple = pieces == 1 and bin_parts == 1
    if simple:
        sent = white.reshape(devices, channels * spans, 2 * FB)
    else:
        sent = white.reshape(pieces, channel_parts, channels, spans, 2, bin_parts, bin_share)
        sent = sent.transpose(1, 5, 0, 2, 3, 4, 6).reshape(devices, pieces * channels * spans, 2 * bin_share)
    received = lax.all_to_all(sent, AXES, split_axis=0, concat_axis=0, tiled=True)
    row = jnp.concatenate([pair_blocks.reshape(1, 2 * slots), pair_count.reshape(1, 1)], axis=1)
    info = every_owner(lax.optimization_barrier((row, white))[0])
    if simple and channels * spans == 8 and spans == 2:
        cross = cross_fast(received, info, slots, groups).reshape(devices, 8, FB)
    else:
        cross = cross_plain(received, info, slots, groups, spans)
        cross = cross.reshape(owners, slots, 2, pieces, channels, bin_share).transpose(0, 1, 3, 2, 4, 5)
        cross = cross.reshape(devices, 2 * channels, bin_share)
    own = lax.all_to_all(cross, AXES, split_axis=0, concat_axis=0, tiled=True)
    rows = block // pieces
    if not (simple and channels == 4):
        own = own.reshape(channel_parts, bin_parts, 2, channels, bin_share).transpose(0, 3, 2, 1, 4)
        own = own.reshape(rows // 4, 4, 2, FB).transpose(0, 2, 1, 3)
    return inverse(own.reshape(2 * rows, FB), scale)


def solution(mesh):
    return jax.shard_map(
        on_device,
        mesh=mesh,
        in_specs=(P("chan", "tm", None), P("chan", None), P("chan")),
        out_specs=P(("chan", "tm"), None),
        check_vma=False,
    )
```

```python
import functools
import math

import jax
import jax.numpy as jnp
import numpy as np
from jax import lax
from jax.experimental import pallas as pl
from jax.experimental.pallas import tpu as pltpu
from jax.sharding import PartitionSpec as P

NS = 4096
FB = 1024
F_LO = 64
LAGS = 2048
AXES = ("chan", "tm")

TURN = 4
QUARTER = NS // TURN
GROUP = FB // TURN
STEP = 32
VMEM = 28 * 1024 * 1024


def bins():
    return np.concatenate([F_LO + g + TURN * np.arange(GROUP) for g in range(TURN)])


def wave(first, second):
    angle = 2.0 * np.pi * (np.multiply.outer(first, second) % NS) / NS
    return np.cos(angle).astype(np.float32), np.sin(angle).astype(np.float32)


def forward_seeds():
    coarse = wave(STEP * np.arange(QUARTER // STEP), bins())
    fine = wave(np.arange(STEP), bins())
    return np.concatenate(coarse + fine).reshape(-1, TURN, GROUP).swapaxes(0, 1).copy()


def inverse_seeds():
    lags = np.arange(LAGS // 2) - LAGS // 2
    coarse = wave(bins()[::STEP], lags)
    fine = wave(TURN * np.arange(STEP), lags)
    return np.concatenate(coarse + fine)


def forward_kernel(x_hbm, seeds_hbm, out_hbm, x, seeds, table, left, spec, out, seed_sem, x_sem, out_sem):
    rows, parts = spec.shape[0], x_sem.shape[0]
    channels = x.shape[0] // parts
    seed_copies = [pltpu.make_async_copy(seeds_hbm.at[g], seeds.at[g], seed_sem.at[g]) for g in range(TURN)]
    x_copies = []
    for k in range(parts):
        at = pl.ds(k * channels, channels)
        x_copies.append(pltpu.make_async_copy(x_hbm.at[at], x.at[at], x_sem.at[k]))
    order = (1, 3, 0, 2)
    for g, copy in zip(order, x_copies):
        seed_copies[g].start()
        copy.start()
    coarse = QUARTER // STEP

    def fill(g):
        seed_copies[g].wait()
        fc, fs = seeds[g, 2 * coarse : 2 * coarse + STEP, :], seeds[g, 2 * coarse + STEP :, :]
        for i in range(coarse):
            c, s = seeds[g, i : i + 1, :], seeds[g, coarse + i : coarse + i + 1, :]
            at = slice(i * STEP, (i + 1) * STEP)
            table[g, at, :GROUP] = (c * fc - s * fs).astype(jnp.bfloat16)
            table[g, at, GROUP:] = -(s * fc + c * fs).astype(jnp.bfloat16)

    for g in order:
        fill(g)
    lanes = QUARTER
    for k, copy in enumerate(x_copies):
        copy.wait()
        here = slice(k * rows // parts, (k + 1) * rows // parts)
        for m in range(TURN):
            quarter = x[k * channels : (k + 1) * channels, :, m * QUARTER : (m + 1) * QUARTER].reshape(rows // parts, QUARTER)
            left[m, here, :] = quarter
            if m:
                left[TURN + m, here, :] = -quarter

    def add_quarters():
        for offset in range(0, QUARTER, lanes):
            into = slice(offset, offset + lanes)
            quarters = [left[m, :, into].astype(jnp.float32) for m in range(TURN)]
            even, odd = quarters[0] + quarters[2], quarters[1] + quarters[3]
            for k, value in enumerate((even + odd, even - odd)):
                high = value.astype(jnp.bfloat16)
                left[2 * TURN + 2 * k, :, into] = high
                left[2 * TURN + 2 * k + 1, :, into] = (value - high.astype(jnp.float32)).astype(jnp.bfloat16)

    power = jnp.zeros((rows, GROUP), jnp.float32)
    for place, g in enumerate(order):
        if place == 2:
            add_quarters()
        cosine, sine = table[g, :, :GROUP], table[g, :, GROUP:]
        turn = (F_LO + g) % TURN
        if turn % 2 == 0:
            pair = jnp.concatenate([left[2 * TURN + turn], left[2 * TURN + turn + 1]], axis=1)
            real = jnp.dot(pair, jnp.concatenate([cosine] * 2, axis=0), preferred_element_type=jnp.float32)
            imag = jnp.dot(pair, jnp.concatenate([sine] * 2, axis=0), preferred_element_type=jnp.float32)
        else:
            ahead = (0, 1, TURN + 2, TURN + 3) if turn == 1 else (0, TURN + 1, TURN + 2, 3)
            behind = (0, TURN + 1, TURN + 2, 3) if turn == 1 else (0, 1, TURN + 2, TURN + 3)
            real = jnp.dot(
                jnp.concatenate([left[k] for k in ahead], axis=1),
                jnp.concatenate([cosine, sine] * 2, axis=0),
                preferred_element_type=jnp.float32,
            )
            imag = jnp.dot(
                jnp.concatenate([left[k] for k in behind], axis=1),
                jnp.concatenate([sine, cosine] * 2, axis=0),
                preferred_element_type=jnp.float32,
            )
        spec[:, g * GROUP : (g + 1) * GROUP] = real
        spec[:, FB + g * GROUP : FB + (g + 1) * GROUP] = imag
        power = power + real * real + imag * imag
    scale = lax.rsqrt(jnp.sum(power, axis=1, keepdims=True) / FB + 1e-06)
    out_copies = []
    pieces = out_sem.shape[0]
    for k in range(pieces):
        at = slice(k * rows // pieces, (k + 1) * rows // pieces)
        out[at, :] = (spec[at, :] * scale[at, :]).astype(jnp.bfloat16)
        out_copies.append(pltpu.make_async_copy(out.at[at], out_hbm.at[at], out_sem.at[k]))
        out_copies[-1].start()
    for copy in out_copies:
        copy.wait()


def in_hbm(array):
    return pltpu.with_memory_space_constraint(array, pltpu.HBM)


def forward(traces):
    rows = traces.shape[0] * traces.shape[1]
    seeds = forward_seeds()
    return pl.pallas_call(
        forward_kernel,
        out_shape=jax.ShapeDtypeStruct((rows, 2 * FB), jnp.bfloat16),
        in_specs=[pl.BlockSpec(memory_space=pltpu.HBM)] * 2,
        out_specs=pl.BlockSpec(memory_space=pltpu.HBM),
        scratch_shapes=[
            pltpu.VMEM(traces.shape, jnp.bfloat16),
            pltpu.VMEM(seeds.shape, jnp.float32),
            pltpu.VMEM((TURN, QUARTER, 2 * GROUP), jnp.bfloat16),
            pltpu.VMEM((3 * TURN, rows, QUARTER), jnp.bfloat16),
            pltpu.VMEM((rows, 2 * FB), jnp.float32),
            pltpu.VMEM((rows, 2 * FB), jnp.bfloat16),
            pltpu.SemaphoreType.DMA((TURN,)),
            pltpu.SemaphoreType.DMA((4,)),
            pltpu.SemaphoreType.DMA((4,)),
        ],
        compiler_params=pltpu.CompilerParams(vmem_limit_bytes=VMEM),
        cost_estimate=pl.CostEstimate(
            flops=2 * rows * NS * 2 * FB, bytes_accessed=2 * rows * (NS + 2 * FB), transcendentals=0
        ),
        name="forward",
    )(in_hbm(traces), in_hbm(jnp.asarray(seeds)))


def cross_kernel(slots, groups, info, received, out, w, total):
    owners = received.shape[0] // groups
    half = out.shape[1]
    lanes = 256
    w[...] = received[...].astype(jnp.float32)

    def one(pair, carry):
        owner, slot = pair // slots, pair % slots
        first = pl.ds(info[owner, 2 * slot] * groups, groups)
        second = pl.ds(info[owner, 2 * slot + 1] * groups, groups)
        alive = jnp.where(slot < info[owner, 2 * slots], 1.0, 0.0)
        at_re = pl.ds(pl.multiple_of(pair * 16, 16), 8)
        at_im = pl.ds(pl.multiple_of(pair * 16 + 8, 8), 8)
        for offset in range(0, half, lanes):
            re = slice(offset, offset + lanes)
            im = slice(half + offset, half + offset + lanes)
            re_a, im_a, re_b, im_b = w[first, :, re], w[first, :, im], w[second, :, re], w[second, :, im]
            sum_re = jnp.sum(re_a * re_b + im_a * im_b, axis=0) * alive
            sum_im = jnp.sum(im_a * re_b - re_a * im_b, axis=0) * alive
            for k in range(0, lanes, 128):
                total[(offset + k) // 128, at_re, :] = sum_re[:, k : k + 128]
                total[(offset + k) // 128, at_im, :] = sum_im[:, k : k + 128]
        return carry

    lax.fori_loop(0, owners * slots, one, 0, unroll=4)
    count = out.shape[0]
    for k in range(half // 128):
        even, odd = total[k, pl.ds(0, count, stride=2), :], total[k, pl.ds(1, count, stride=2), :]
        out[:, k * 128 : (k + 1) * 128] = (even + odd).astype(jnp.bfloat16)


def cross_fast(received, info, slots, groups):
    owners = received.shape[0] // groups
    half = received.shape[2] // 2
    vmem = pl.BlockSpec(memory_space=pltpu.VMEM)
    rows = owners * slots * 8
    return pl.pallas_call(
        functools.partial(cross_kernel, slots, groups),
        out_shape=jax.ShapeDtypeStruct((rows, half), jnp.bfloat16),
        in_specs=[pl.BlockSpec(memory_space=pltpu.SMEM), vmem],
        out_specs=vmem,
        scratch_shapes=[
            pltpu.VMEM(received.shape, jnp.float32),
            pltpu.VMEM((half // 128, 2 * rows, 128), jnp.float32),
        ],
        compiler_params=pltpu.CompilerParams(vmem_limit_bytes=VMEM),
        cost_estimate=pl.CostEstimate(
            flops=8 * rows * 8 * half, bytes_accessed=2 * received.size + 2 * rows * half, transcendentals=0
        ),
        name="cross",
    )(info, received)


def cross_plain(received, info, slots, groups, spans):
    half = received.shape[2] // 2
    owners = received.shape[0] // groups
    channels = received.shape[1] // spans
    pairs = info[:, : 2 * slots].reshape(owners * slots, 2)
    alive = (lax.iota(jnp.int32, slots)[None, :] < info[:, 2 * slots][:, None]).astype(jnp.float32).reshape(-1)
    blocks = received.reshape(owners, groups, channels, spans, 2, half)

    def one(inputs):
        pair, live = inputs
        first, second = blocks[pair[0]].astype(jnp.float32), blocks[pair[1]].astype(jnp.float32)
        re_a, im_a, re_b, im_b = first[..., 0, :], first[..., 1, :], second[..., 0, :], second[..., 1, :]
        cross_re = jnp.sum(re_a * re_b + im_a * im_b, axis=(0, 2))
        cross_im = jnp.sum(im_a * re_b - re_a * im_b, axis=(0, 2))
        return (jnp.stack([cross_re, cross_im]) * live).astype(jnp.bfloat16)

    return lax.map(one, (pairs, alive))


def every_owner(row):
    owners = lax.axis_size("chan")
    ring = row
    while ring.shape[0] < owners:
        hop = ring.shape[0]
        more = lax.ppermute(ring, "chan", [(source, (source - hop) % owners) for source in range(owners)])
        ring = jnp.concatenate([ring, more])[:owners]
    return jnp.roll(ring, lax.axis_index("chan"), axis=0)


def inverse_kernel(scale, y, seeds, out_hbm, out, ordered, table, sem):
    rows = y.shape[0]
    half = LAGS // 2
    coarse = FB // STEP
    lanes = 256
    target = lax.broadcasted_iota(jnp.int32, (rows, rows), 0)
    source = lax.broadcasted_iota(jnp.int32, (rows, rows), 1)
    wanted = source // 8 * 4 + source % 4 + source // 4 % 2 * (rows // 2)
    pick = jnp.where(target == wanted, 1.0, 0.0).astype(jnp.bfloat16)
    for g in range(TURN):
        columns = slice(g * GROUP, (g + 1) * GROUP)
        moved = jnp.dot(pick, y[:, columns], preferred_element_type=jnp.float32)
        real, imag = moved[: rows // 2], moved[rows // 2 :]
        far = [(real, imag), (-imag, real), (-real, -imag), (imag, -real)][(F_LO + g) % TURN]
        for k, (near_side, far_side) in enumerate(zip((real, imag), far)):
            into = slice(k * FB + g * GROUP, k * FB + (g + 1) * GROUP)
            ordered[: rows // 2, into] = near_side.astype(jnp.bfloat16)
            ordered[rows // 2 :, into] = far_side.astype(jnp.bfloat16)
    copies = []
    for k, offset in enumerate(range(0, half, lanes)):
        columns = slice(offset, offset + lanes)
        fc, fs = seeds[2 * coarse : 2 * coarse + STEP, columns], seeds[2 * coarse + STEP :, columns]
        for i in range(coarse):
            c, s = seeds[i : i + 1, columns], seeds[coarse + i : coarse + i + 1, columns]
            table[k % 2, i * STEP : (i + 1) * STEP, :] = (c * fc - s * fs).astype(jnp.bfloat16)
            table[k % 2, FB + i * STEP : FB + (i + 1) * STEP, :] = -(s * fc + c * fs).astype(jnp.bfloat16)
        product = jnp.dot(ordered[...], table[k % 2], preferred_element_type=jnp.float32) * scale
        for side in range(2):
            at = slice(side * half + offset, side * half + offset + lanes)
            out[:, at] = product[side * rows // 2 : (side + 1) * rows // 2]
            copies.append(pltpu.make_async_copy(out.at[:, at], out_hbm.at[:, at], sem.at[2 * k + side]))
            copies[-1].start()
    for copy in copies:
        copy.wait()


def inverse(y, scale):
    rows = y.shape[0]
    seeds = inverse_seeds()
    vmem = pl.BlockSpec(memory_space=pltpu.VMEM)
    return pl.pallas_call(
        functools.partial(inverse_kernel, scale),
        out_shape=jax.ShapeDtypeStruct((rows // 2, LAGS), jnp.float32),
        in_specs=[vmem] * 2,
        out_specs=pl.BlockSpec(memory_space=pltpu.HBM),
        scratch_shapes=[
            pltpu.VMEM((rows // 2, LAGS), jnp.float32),
            pltpu.VMEM((rows, 2 * FB), jnp.bfloat16),
            pltpu.VMEM((2, 2 * FB, 256), jnp.bfloat16),
            pltpu.SemaphoreType.DMA((LAGS // 256,)),
        ],
        compiler_params=pltpu.CompilerParams(vmem_limit_bytes=VMEM),
        cost_estimate=pl.CostEstimate(
            flops=2 * rows * FB * LAGS, bytes_accessed=2 * rows * FB + 2 * rows * LAGS, transcendentals=0
        ),
        name="inverse",
    )(y, jnp.asarray(seeds))


def on_device(traces, pair_blocks, pair_count):
    owners, groups = lax.axis_size("chan"), lax.axis_size("tm")
    devices = owners * groups
    block, spans = traces.shape[0], traces.shape[1]
    slots = pair_blocks.shape[0]
    pieces = groups // slots
    channel_parts = min(devices, block // pieces)
    bin_parts = devices // channel_parts
    channels = block // pieces // channel_parts
    bin_share = FB // bin_parts
    scale = 1.0 / math.sqrt(FB * spans * groups)

    white = forward(traces)
    simple = pieces == 1 and bin_parts == 1
    if simple:
        sent = white.reshape(devices, channels * spans, 2 * FB)
    else:
        sent = white.reshape(pieces, channel_parts, channels, spans, 2, bin_parts, bin_share)
        sent = sent.transpose(1, 5, 0, 2, 3, 4, 6).reshape(devices, pieces * channels * spans, 2 * bin_share)
    received = lax.all_to_all(sent, AXES, split_axis=0, concat_axis=0, tiled=True)
    row = jnp.concatenate([pair_blocks.reshape(1, 2 * slots), pair_count.reshape(1, 1)], axis=1)
    info = every_owner(lax.optimization_barrier((row, white))[0])
    if simple and channels * spans == 8 and spans == 2:
        cross = cross_fast(received, info, slots, groups).reshape(devices, 8, FB)
    else:
        cross = cross_plain(received, info, slots, groups, spans)
        cross = cross.reshape(owners, slots, 2, pieces, channels, bin_share).transpose(0, 1, 3, 2, 4, 5)
        cross = cross.reshape(devices, 2 * channels, bin_share)
    own = lax.all_to_all(cross, AXES, split_axis=0, concat_axis=0, tiled=True)
    rows = block // pieces
    if not (simple and channels == 4):
        own = own.reshape(channel_parts, bin_parts, 2, channels, bin_share).transpose(0, 3, 2, 1, 4)
        own = own.reshape(rows // 4, 4, 2, FB).transpose(0, 2, 1, 3)
    return inverse(own.reshape(2 * rows, FB), scale)


def solution(mesh):
    return jax.shard_map(
        on_device,
        mesh=mesh,
        in_specs=(P("chan", "tm", None), P("chan", None), P("chan")),
        out_specs=P(("chan", "tm"), None),
        check_vma=False,
    )
```

```python
import functools
import math

import jax
import jax.numpy as jnp
import numpy as np
from jax import lax
from jax.experimental import pallas as pl
from jax.experimental.pallas import tpu as pltpu
from jax.sharding import PartitionSpec as P

NS = 4096
FB = 1024
F_LO = 64
LAGS = 2048
AXES = ("chan", "tm")

TURN = 4
QUARTER = NS // TURN
GROUP = FB // TURN
STEP = 32
VMEM = 28 * 1024 * 1024


def bins():
    return np.concatenate([F_LO + g + TURN * np.arange(GROUP) for g in range(TURN)])


def wave(first, second):
    angle = 2.0 * np.pi * (np.multiply.outer(first, second) % NS) / NS
    return np.cos(angle).astype(np.float32), np.sin(angle).astype(np.float32)


def forward_seeds():
    coarse = wave(STEP * np.arange(QUARTER // STEP), bins())
    fine = wave(np.arange(STEP), bins())
    return np.concatenate(coarse + fine).reshape(-1, TURN, GROUP).swapaxes(0, 1).copy()


def inverse_seeds():
    lags = np.arange(LAGS // 2) - LAGS // 2
    coarse = wave(bins()[::STEP], lags)
    fine = wave(TURN * np.arange(STEP), lags)
    return np.concatenate(coarse + fine)


def forward_kernel(x_hbm, seeds_hbm, out_hbm, x, seeds, table, left, spec, out, seed_sem, x_sem, out_sem):
    rows, parts = spec.shape[0], x_sem.shape[0]
    channels = x.shape[0] // parts
    seed_copies = [pltpu.make_async_copy(seeds_hbm.at[g], seeds.at[g], seed_sem.at[g]) for g in range(TURN)]
    x_copies = []
    for k in range(parts):
        at = pl.ds(k * channels, channels)
        x_copies.append(pltpu.make_async_copy(x_hbm.at[at], x.at[at], x_sem.at[k]))
    order = (1, 3, 0, 2)
    for g, copy in zip(order, x_copies):
        seed_copies[g].start()
        copy.start()
    coarse = QUARTER // STEP

    def fill(g):
        seed_copies[g].wait()
        fc, fs = seeds[g, 2 * coarse : 2 * coarse + STEP, :], seeds[g, 2 * coarse + STEP :, :]
        for i in range(coarse):
            c, s = seeds[g, i : i + 1, :], seeds[g, coarse + i : coarse + i + 1, :]
            at = slice(i * STEP, (i + 1) * STEP)
            table[g, at, :GROUP] = (c * fc - s * fs).astype(jnp.bfloat16)
            table[g, at, GROUP:] = -(s * fc + c * fs).astype(jnp.bfloat16)

    for g in order:
        fill(g)
    lanes = QUARTER
    for k, copy in enumerate(x_copies):
        copy.wait()
        here = slice(k * rows // parts, (k + 1) * rows // parts)
        for m in range(TURN):
            quarter = x[k * channels : (k + 1) * channels, :, m * QUARTER : (m + 1) * QUARTER].reshape(rows // parts, QUARTER)
            left[m, here, :] = quarter
            if m:
                left[TURN + m, here, :] = -quarter

    def add_quarters():
        for offset in range(0, QUARTER, lanes):
            into = slice(offset, offset + lanes)
            quarters = [left[m, :, into].astype(jnp.float32) for m in range(TURN)]
            even, odd = quarters[0] + quarters[2], quarters[1] + quarters[3]
            for k, value in enumerate((even + odd, even - odd)):
                high = value.astype(jnp.bfloat16)
                left[2 * TURN + 2 * k, :, into] = high
                left[2 * TURN + 2 * k + 1, :, into] = (value - high.astype(jnp.float32)).astype(jnp.bfloat16)

    power = jnp.zeros((rows, GROUP), jnp.float32)
    for place, g in enumerate(order):
        if place == 2:
            add_quarters()
        cosine, sine = table[g, :, :GROUP], table[g, :, GROUP:]
        turn = (F_LO + g) % TURN
        if turn % 2 == 0:
            pair = jnp.concatenate([left[2 * TURN + turn], left[2 * TURN + turn + 1]], axis=1)
            real = jnp.dot(pair, jnp.concatenate([cosine] * 2, axis=0), preferred_element_type=jnp.float32)
            imag = jnp.dot(pair, jnp.concatenate([sine] * 2, axis=0), preferred_element_type=jnp.float32)
        else:
            ahead = (0, 1, TURN + 2, TURN + 3) if turn == 1 else (0, TURN + 1, TURN + 2, 3)
            behind = (0, TURN + 1, TURN + 2, 3) if turn == 1 else (0, 1, TURN + 2, TURN + 3)
            real = jnp.dot(
                jnp.concatenate([left[k] for k in ahead], axis=1),
                jnp.concatenate([cosine, sine] * 2, axis=0),
                preferred_element_type=jnp.float32,
            )
            imag = jnp.dot(
                jnp.concatenate([left[k] for k in behind], axis=1),
                jnp.concatenate([sine, cosine] * 2, axis=0),
                preferred_element_type=jnp.float32,
            )
        spec[:, g * GROUP : (g + 1) * GROUP] = real
        spec[:, FB + g * GROUP : FB + (g + 1) * GROUP] = imag
        power = power + real * real + imag * imag
    scale = lax.rsqrt(jnp.sum(power, axis=1, keepdims=True) / FB + 1e-06)
    out_copies = []
    pieces = out_sem.shape[0]
    for k in range(pieces):
        at = slice(k * rows // pieces, (k + 1) * rows // pieces)
        out[at, :] = (spec[at, :] * scale[at, :]).astype(jnp.bfloat16)
        out_copies.append(pltpu.make_async_copy(out.at[at], out_hbm.at[at], out_sem.at[k]))
        out_copies[-1].start()
    for copy in out_copies:
        copy.wait()


def in_hbm(array):
    return pltpu.with_memory_space_constraint(array, pltpu.HBM)


def forward(traces):
    rows = traces.shape[0] * traces.shape[1]
    seeds = forward_seeds()
    return pl.pallas_call(
        forward_kernel,
        out_shape=jax.ShapeDtypeStruct((rows, 2 * FB), jnp.bfloat16),
        in_specs=[pl.BlockSpec(memory_space=pltpu.HBM)] * 2,
        out_specs=pl.BlockSpec(memory_space=pltpu.HBM),
        scratch_shapes=[
            pltpu.VMEM(traces.shape, jnp.bfloat16),
            pltpu.VMEM(seeds.shape, jnp.float32),
            pltpu.VMEM((TURN, QUARTER, 2 * GROUP), jnp.bfloat16),
            pltpu.VMEM((3 * TURN, rows, QUARTER), jnp.bfloat16),
            pltpu.VMEM((rows, 2 * FB), jnp.float32),
            pltpu.VMEM((rows, 2 * FB), jnp.bfloat16),
            pltpu.SemaphoreType.DMA((TURN,)),
            pltpu.SemaphoreType.DMA((4,)),
            pltpu.SemaphoreType.DMA((4,)),
        ],
        compiler_params=pltpu.CompilerParams(vmem_limit_bytes=VMEM),
        cost_estimate=pl.CostEstimate(
            flops=2 * rows * NS * 2 * FB, bytes_accessed=2 * rows * (NS + 2 * FB), transcendentals=0
        ),
        name="forward",
    )(in_hbm(traces), in_hbm(jnp.asarray(seeds)))


def cross_kernel(slots, groups, info_any, received, out, w, total, info, sem):
    owners = received.shape[0] // groups
    half = out.shape[1]
    lanes = 256
    copy = pltpu.make_async_copy(info_any, info, sem)
    copy.start()
    w[...] = received[...].astype(jnp.float32)
    copy.wait()

    def one(pair, carry):
        owner, slot = pair // slots, pair % slots
        first = pl.ds(info[owner, 2 * slot] * groups, groups)
        second = pl.ds(info[owner, 2 * slot + 1] * groups, groups)
        alive = jnp.where(slot < info[owner, 2 * slots], 1.0, 0.0)
        at_re = pl.ds(pl.multiple_of(pair * 16, 16), 8)
        at_im = pl.ds(pl.multiple_of(pair * 16 + 8, 8), 8)
        for offset in range(0, half, lanes):
            re = slice(offset, offset + lanes)
            im = slice(half + offset, half + offset + lanes)
            re_a, im_a, re_b, im_b = w[first, :, re], w[first, :, im], w[second, :, re], w[second, :, im]
            sum_re = jnp.sum(re_a * re_b + im_a * im_b, axis=0) * alive
            sum_im = jnp.sum(im_a * re_b - re_a * im_b, axis=0) * alive
            for k in range(0, lanes, 128):
                total[(offset + k) // 128, at_re, :] = sum_re[:, k : k + 128]
                total[(offset + k) // 128, at_im, :] = sum_im[:, k : k + 128]
        return carry

    lax.fori_loop(0, owners * slots, one, 0, unroll=8)
    count = out.shape[0]
    for k in range(half // 128):
        even, odd = total[k, pl.ds(0, count, stride=2), :], total[k, pl.ds(1, count, stride=2), :]
        out[:, k * 128 : (k + 1) * 128] = (even + odd).astype(jnp.bfloat16)


def cross_fast(received, info, slots, groups):
    owners = received.shape[0] // groups
    half = received.shape[2] // 2
    vmem = pl.BlockSpec(memory_space=pltpu.VMEM)
    rows = owners * slots * 8
    return pl.pallas_call(
        functools.partial(cross_kernel, slots, groups),
        out_shape=jax.ShapeDtypeStruct((rows, half), jnp.bfloat16),
        in_specs=[pl.BlockSpec(memory_space=pl.ANY), vmem],
        out_specs=vmem,
        scratch_shapes=[
            pltpu.VMEM(received.shape, jnp.float32),
            pltpu.VMEM((half // 128, 2 * rows, 128), jnp.float32),
            pltpu.SMEM(info.shape, jnp.int32),
            pltpu.SemaphoreType.DMA,
        ],
        compiler_params=pltpu.CompilerParams(vmem_limit_bytes=VMEM),
        cost_estimate=pl.CostEstimate(
            flops=8 * rows * 8 * half, bytes_accessed=2 * received.size + 2 * rows * half, transcendentals=0
        ),
        name="cross",
    )(info, received)


def cross_plain(received, info, slots, groups, spans):
    half = received.shape[2] // 2
    owners = received.shape[0] // groups
    channels = received.shape[1] // spans
    pairs = info[:, : 2 * slots].reshape(owners * slots, 2)
    alive = (lax.iota(jnp.int32, slots)[None, :] < info[:, 2 * slots][:, None]).astype(jnp.float32).reshape(-1)
    blocks = received.reshape(owners, groups, channels, spans, 2, half)

    def one(inputs):
        pair, live = inputs
        first, second = blocks[pair[0]].astype(jnp.float32), blocks[pair[1]].astype(jnp.float32)
        re_a, im_a, re_b, im_b = first[..., 0, :], first[..., 1, :], second[..., 0, :], second[..., 1, :]
        cross_re = jnp.sum(re_a * re_b + im_a * im_b, axis=(0, 2))
        cross_im = jnp.sum(im_a * re_b - re_a * im_b, axis=(0, 2))
        return (jnp.stack([cross_re, cross_im]) * live).astype(jnp.bfloat16)

    return lax.map(one, (pairs, alive))


def every_owner(row):
    owners = lax.axis_size("chan")
    ring = row
    while ring.shape[0] < owners:
        hop = ring.shape[0]
        more = lax.ppermute(ring, "chan", [(source, (source - hop) % owners) for source in range(owners)])
        ring = jnp.concatenate([ring, more])[:owners]
    return jnp.roll(ring, lax.axis_index("chan"), axis=0)


def inverse_kernel(scale, y, seeds, out_hbm, out, ordered, table, sem):
    rows = y.shape[0]
    half = LAGS // 2
    coarse = FB // STEP
    lanes = 256
    target = lax.broadcasted_iota(jnp.int32, (rows, rows), 0)
    source = lax.broadcasted_iota(jnp.int32, (rows, rows), 1)
    wanted = source // 8 * 4 + source % 4 + source // 4 % 2 * (rows // 2)
    pick = jnp.where(target == wanted, 1.0, 0.0).astype(jnp.bfloat16)
    for g in range(TURN):
        columns = slice(g * GROUP, (g + 1) * GROUP)
        moved = jnp.dot(pick, y[:, columns], preferred_element_type=jnp.float32)
        real, imag = moved[: rows // 2], moved[rows // 2 :]
        far = [(real, imag), (-imag, real), (-real, -imag), (imag, -real)][(F_LO + g) % TURN]
        for k, (near_side, far_side) in enumerate(zip((real, imag), far)):
            into = slice(k * FB + g * GROUP, k * FB + (g + 1) * GROUP)
            ordered[: rows // 2, into] = near_side.astype(jnp.bfloat16)
            ordered[rows // 2 :, into] = far_side.astype(jnp.bfloat16)
    copies = []
    for k, offset in enumerate(range(0, half, lanes)):
        columns = slice(offset, offset + lanes)
        fc, fs = seeds[2 * coarse : 2 * coarse + STEP, columns], seeds[2 * coarse + STEP :, columns]
        for i in range(coarse):
            c, s = seeds[i : i + 1, columns], seeds[coarse + i : coarse + i + 1, columns]
            table[k % 2, i * STEP : (i + 1) * STEP, :] = (c * fc - s * fs).astype(jnp.bfloat16)
            table[k % 2, FB + i * STEP : FB + (i + 1) * STEP, :] = -(s * fc + c * fs).astype(jnp.bfloat16)
        product = jnp.dot(ordered[...], table[k % 2], preferred_element_type=jnp.float32) * scale
        for side in range(2):
            at = slice(side * half + offset, side * half + offset + lanes)
            out[:, at] = product[side * rows // 2 : (side + 1) * rows // 2]
            copies.append(pltpu.make_async_copy(out.at[:, at], out_hbm.at[:, at], sem.at[2 * k + side]))
            copies[-1].start()
    for copy in copies:
        copy.wait()


def inverse(y, scale):
    rows = y.shape[0]
    seeds = inverse_seeds()
    vmem = pl.BlockSpec(memory_space=pltpu.VMEM)
    return pl.pallas_call(
        functools.partial(inverse_kernel, scale),
        out_shape=jax.ShapeDtypeStruct((rows // 2, LAGS), jnp.float32),
        in_specs=[vmem] * 2,
        out_specs=pl.BlockSpec(memory_space=pltpu.HBM),
        scratch_shapes=[
            pltpu.VMEM((rows // 2, LAGS), jnp.float32),
            pltpu.VMEM((rows, 2 * FB), jnp.bfloat16),
            pltpu.VMEM((2, 2 * FB, 256), jnp.bfloat16),
            pltpu.SemaphoreType.DMA((LAGS // 256,)),
        ],
        compiler_params=pltpu.CompilerParams(vmem_limit_bytes=VMEM),
        cost_estimate=pl.CostEstimate(
            flops=2 * rows * FB * LAGS, bytes_accessed=2 * rows * FB + 2 * rows * LAGS, transcendentals=0
        ),
        name="inverse",
    )(y, jnp.asarray(seeds))


def on_device(traces, pair_blocks, pair_count):
    owners, groups = lax.axis_size("chan"), lax.axis_size("tm")
    devices = owners * groups
    block, spans = traces.shape[0], traces.shape[1]
    slots = pair_blocks.shape[0]
    pieces = groups // slots
    channel_parts = min(devices, block // pieces)
    bin_parts = devices // channel_parts
    channels = block // pieces // channel_parts
    bin_share = FB // bin_parts
    scale = 1.0 / math.sqrt(FB * spans * groups)

    white = forward(traces)
    simple = pieces == 1 and bin_parts == 1
    if simple:
        sent = white.reshape(devices, channels * spans, 2 * FB)
    else:
        sent = white.reshape(pieces, channel_parts, channels, spans, 2, bin_parts, bin_share)
        sent = sent.transpose(1, 5, 0, 2, 3, 4, 6).reshape(devices, pieces * channels * spans, 2 * bin_share)
    received = lax.all_to_all(sent, AXES, split_axis=0, concat_axis=0, tiled=True)
    row = jnp.concatenate([pair_blocks.reshape(1, 2 * slots), pair_count.reshape(1, 1)], axis=1)
    info = every_owner(lax.optimization_barrier((row, white))[0])
    if simple and channels * spans == 8 and spans == 2:
        cross = cross_fast(received, info, slots, groups).reshape(devices, 8, FB)
    else:
        cross = cross_plain(received, info, slots, groups, spans)
        cross = cross.reshape(owners, slots, 2, pieces, channels, bin_share).transpose(0, 1, 3, 2, 4, 5)
        cross = cross.reshape(devices, 2 * channels, bin_share)
    own = lax.all_to_all(cross, AXES, split_axis=0, concat_axis=0, tiled=True)
    rows = block // pieces
    if not (simple and channels == 4):
        own = own.reshape(channel_parts, bin_parts, 2, channels, bin_share).transpose(0, 3, 2, 1, 4)
        own = own.reshape(rows // 4, 4, 2, FB).transpose(0, 2, 1, 3)
    return inverse(own.reshape(2 * rows, FB), scale)


def solution(mesh):
    return jax.shard_map(
        on_device,
        mesh=mesh,
        in_specs=(P("chan", "tm", None), P("chan", None), P("chan")),
        out_specs=P(("chan", "tm"), None),
        check_vma=False,
    )
```
